32 devices in a mesh: groups: 2 (over y), shard: 4 (over z), section: 2 (over x), halo: 2 (over core).
Axes of the slice: x: 2, y: 2, z: 4, core: 2. Of those that a mesh axis runs over, the one named last changes fastest.
Arguments:
- features: bfloat16 [4, 4, 16, 64, 320], P(('groups', 'section'), 'shard', 'halo'), parts along dimension 0, may hold values from -6 to 6
- timesteps: int32 [4, 2], P(('groups', 'section')), parts along dimension 0, may hold values from 0 to 999
- conv_first: bfloat16 [2, 3, 3, 320, 320], P('section'), may hold values from -0.109375 to 0.109375
- conv_second: bfloat16 [2, 3, 3, 320, 320], P('section'), may hold values from -0.109375 to 0.109375
- time_weight: bfloat16 [2, 320, 320], P('section'), may hold values from -0.3125 to 0.3125
- qkv_weight: bfloat16 [2, 320, 960], P('section'), may hold values from -7 to 7
- attn_out: bfloat16 [2, 320, 320], P('section'), may hold values from -0.3125 to 0.3125
- geglu_in: bfloat16 [2, 320, 2560], P('section'), may hold values from -0.3125 to 0.3125
- geglu_out: bfloat16 [2, 1280, 320], P('section'), may hold values from -0.15625 to 0.15625
Outputs:
- result: bfloat16 [4, 4, 16, 64, 320], P(('groups', 'section'), 'shard', 'halo'), parts along dimension 0
The draws below stay inside these ranges and needn't reach their ends.
There are 2 independent parts, one for each index of `groups`. The reference program is written for one: setup_inputs(seed, part) draws one part's arguments, and reference() takes and returns one part's arrays. A program takes and returns all parts, laid end to end along the dimension named above; an argument that names none is the same for every part. Nothing has to cross between parts.
All inputs are finite; a program needn't handle non-finite values.
Results may differ from the reference program's by a relative error of at most 0.02.
Values may be sent and summed in bfloat16 or wider, within the bound.
A program may use at most 64 MiB of HBM per device.

```python
import math
import jax
import jax.numpy as jnp
from jax import lax

C = 320
HEAD_DIM = 64
FF = 1280
GROUPS = 32
WIDTH = 64
STEPS = 2
SECTIONS = 2
FRAMES = 4
HEIGHT = 16


def draw_qkv_weight(key, part):
    first_key, second_key, third_key = jax.random.split(jax.random.fold_in(key, 7), 3)
    scaling = C ** (-0.5)
    key_weight = jax.random.truncated_normal(second_key, -4.0, 4.0, (SECTIONS, C, C), jnp.float32) * scaling
    value_weight = jax.random.truncated_normal(third_key, -4.0, 4.0, (SECTIONS, C, C), jnp.float32) * scaling
    noise_weight = jax.random.truncated_normal(first_key, -4.0, 4.0, (SECTIONS, C, C), jnp.float32) * scaling
    query_weight = noise_weight
    return jnp.concatenate([query_weight, key_weight, value_weight], axis=2).astype(jnp.bfloat16)


def set_ends(drawn, own_key, low, largest):
    extent = drawn.shape
    spot = [jax.random.randint(jax.random.fold_in(own_key, axis), (), 0, extent[axis]) for axis in range(len(extent))]
    drawn = drawn.at[tuple(spot)].set(low)
    longest = extent.index(max(extent))
    spot[longest] = (spot[longest] + 1) % extent[longest]
    return drawn.at[tuple(spot)].set(largest)


def level_of(stream_key, dims, cuts, low, top_value):
    def one(axis_at, parts):
        steps = jax.random.uniform(jax.random.fold_in(jax.random.fold_in(stream_key, 6), axis_at), (parts,), jnp.float32, low / len(cuts), top_value / len(cuts))
        return jnp.repeat(jnp.exp(steps), dims[axis_at] // parts).reshape((-1,) + (1,) * (len(dims) - axis_at - 1))

    loudness = one(*cuts[0])
    for cut in cuts[1:]:
        loudness = loudness * one(*cut)
    return loudness


def gaussian(own_key, shape, scale, bound, pieces=(), kind=jnp.bfloat16):
    factor_of = level_of(own_key, shape, pieces, -0.22, 0.18) if pieces else 1.0
    result = jax.random.normal(own_key, shape, jnp.float32) * scale * factor_of
    return jnp.minimum(jnp.maximum(result, -bound), bound).astype(kind)


def setup_inputs(seed: int = 0, part: int = 0) -> dict:
    splits = jax.random.split(jax.random.key(seed), 10)
    part_keys = jax.random.split(jax.random.fold_in(splits[9], part), 10)
    return {
        "features": gaussian(part_keys[0], (SECTIONS, FRAMES, HEIGHT, WIDTH, C), 1.0, 6.0, ((0, 2), (1, 4), (2, 2))),
        "timesteps": set_ends(jax.random.randint(part_keys[1], (SECTIONS, STEPS), 0, 1000), jax.random.fold_in(part_keys[1], 1), 0, 999).astype(jnp.int32),
        "conv_first": gaussian(splits[2], (SECTIONS, 3, 3, C, C), (9 * C) ** -0.5, 0.109375, ((0, 2),)),
        "conv_second": gaussian(splits[3], (SECTIONS, 3, 3, C, C), (9 * C) ** -0.5, 0.109375, ((0, 2),)),
        "time_weight": gaussian(splits[4], (SECTIONS, C, C), C ** -0.5, 0.3125, ((0, 2),)),
        "qkv_weight": draw_qkv_weight(jax.random.fold_in(splits[9], 71), part),
        "attn_out": gaussian(splits[6], (SECTIONS, C, C), C ** -0.5, 0.3125, ((0, 2),)),
        "geglu_in": gaussian(splits[7], (SECTIONS, C, 2 * FF), C ** -0.5, 0.3125, ((0, 2),)),
        "geglu_out": gaussian(splits[8], (SECTIONS, FF, C), FF ** -0.5, 0.15625, ((0, 2),)),
    }


def norm_silu(field):
    frames, height, column_count, channels = field.shape
    grouped = field.reshape(frames, height * column_count, GROUPS, channels // GROUPS)
    average = lax.optimization_barrier(jnp.mean(grouped, axis=(1, 3), keepdims=True))
    squares = lax.optimization_barrier(jnp.mean(grouped * grouped, axis=(1, 3), keepdims=True))
    normed = (grouped - average) * lax.rsqrt(squares - average * average + 1e-05)
    return jax.nn.silu(normed).reshape(field.shape).astype(jnp.bfloat16)

def conv_frames(active, kernel):
    frames, height, column_count, channels = active.shape
    padded = jnp.pad(active, ((0, 0), (1, 1), (1, 1), (0, 0)))
    outcome = jnp.zeros((frames * height * column_count, kernel.shape[3]), jnp.float32)
    for row_offset in range(3):
        for column_offset in range(3):
            window = padded[:, row_offset:row_offset + height, column_offset:column_offset + column_count, :]
            outcome = outcome + jnp.dot(window.reshape(-1, channels), kernel[row_offset, column_offset], preferred_element_type=jnp.float32)
    return outcome.reshape(frames, height, column_count, kernel.shape[3])

def embed_time(stamp, time_weight):
    half_width = time_weight.shape[0] // 2
    frequency = jnp.exp(-math.log(10000.0) * jnp.arange(half_width, dtype=jnp.float32) / half_width)
    angles = stamp.astype(jnp.float32) * frequency
    sinusoid = jnp.concatenate([jnp.cos(angles), jnp.sin(angles)])
    return jnp.dot(jax.nn.silu(sinusoid).astype(jnp.bfloat16)[None, :], time_weight, preferred_element_type=jnp.float32)[0]

def layer_norm(stream):
    values_f = stream.astype(jnp.float32)
    average = lax.optimization_barrier(jnp.mean(values_f, axis=-1, keepdims=True))
    centred = values_f - average
    spread = lax.optimization_barrier(jnp.mean(centred * centred, axis=-1, keepdims=True))
    return (centred * lax.rsqrt(spread + 1e-05)).astype(jnp.bfloat16)

def attend(query, key_block, value_block):
    query_frames, pixels, channels = query.shape
    head_count = channels // HEAD_DIM

    def split_heads(tensor):
        return tensor.reshape(tensor.shape[0], tensor.shape[1], head_count, HEAD_DIM).astype(jnp.float32)
    scores = jnp.einsum('fphd,gphd->phfg', split_heads(query), split_heads(key_block)) * HEAD_DIM ** (-0.5)
    weights = jax.nn.softmax(scores, axis=-1).astype(jnp.bfloat16)
    mixed = jnp.einsum('phfg,gphd->fphd', weights.astype(jnp.float32), split_heads(value_block))
    return mixed.reshape(query_frames, pixels, channels).astype(jnp.bfloat16)

def temporal(stream, qkv_weight, attn_out):
    frames, pixels, channels = stream.shape
    normed = layer_norm(stream).reshape(-1, channels)
    projected = jnp.dot(normed, qkv_weight, preferred_element_type=jnp.float32).astype(jnp.bfloat16)
    projected = projected.reshape(frames, pixels, 3 * channels)
    mixed = attend(projected[:, :, :channels], projected[:, :, channels:2 * channels], projected[:, :, 2 * channels:])
    update = jnp.dot(mixed.reshape(-1, channels), attn_out, preferred_element_type=jnp.float32).reshape(stream.shape)
    return (stream.astype(jnp.float32) + update).astype(jnp.bfloat16)

def feed(stream, geglu_in, geglu_out):
    channels = stream.shape[2]
    inner = geglu_out.shape[0]
    normed = layer_norm(stream).reshape(-1, channels)
    projected = jnp.dot(normed, geglu_in, preferred_element_type=jnp.float32)
    active = (projected[:, :inner] * jax.nn.gelu(projected[:, inner:], approximate=False)).astype(jnp.bfloat16)
    update = jnp.dot(active, geglu_out, preferred_element_type=jnp.float32).reshape(stream.shape)
    return (stream.astype(jnp.float32) + update).astype(jnp.bfloat16)

def section_block(field, stamp, conv_first, conv_second, time_weight, qkv_weight, attn_out, geglu_in, geglu_out):
    frames, height, column_count, channels = field.shape
    base = field.astype(jnp.float32)
    first = conv_frames(norm_silu(base), conv_first) + embed_time(stamp, time_weight)
    second = conv_frames(norm_silu(first), conv_second)
    stream = (base + second).astype(jnp.bfloat16).reshape(frames, height * column_count, channels)
    stream = temporal(stream, qkv_weight, attn_out)
    stream = feed(stream, geglu_in, geglu_out)
    return stream.reshape(field.shape)

def reference(features, timesteps, conv_first, conv_second, time_weight, qkv_weight, attn_out, geglu_in, geglu_out):
    current = features
    for denoise_step in range(STEPS):
        current = jnp.roll(current, 1, axis=0)
        outputs = []
        for section in range(SECTIONS):
            outputs.append(section_block(current[section], timesteps[section, denoise_step], conv_first[section], conv_second[section], time_weight[section], qkv_weight[section], attn_out[section], geglu_in[section], geglu_out[section]))
        current = jnp.stack(outputs)
    return current
```

```python
import functools
import math

import jax
import jax.numpy as jnp
from jax import lax
from jax.experimental import pallas as pl
from jax.experimental.pallas import tpu as pltpu
from jax.sharding import PartitionSpec as P

HEAD_DIM = 64
GROUPS = 32
STEPS = 2
MESH = pl.DeviceIdType.MESH
F32 = jnp.float32
BF16 = jnp.bfloat16
BLK = 64
SUBS = 2
UNROLL = 4
SHIFTS = 4
PAD = 8


def matmul(a, b):
    return jnp.dot(a, b, preferred_element_type=F32)


def matmul_t(a, b):
    return lax.dot_general(a, b, (((1,), (1,)), ((), ())), preferred_element_type=F32)


def silu(u):
    return u * (1.0 / (1.0 + jnp.exp(-u)))


def kernel(dims, stamps, feat, cf_h, cs_h, tw_h, qkv_h, ao_h, gi_h, go_h, out, *scratch):
    (rows, width, chans, inner, nsh, nsec, subs) = dims
    (F, FX, first_rx, H, G, A, S, PB, O, stat_tx, stat_rx, edge_x, edge_h, emb, gmask, hmask, hmask_t,
     N, Q, K, V, PH, PL, OB, S2, ACT,
     cf, cs, tw, qkv, ao, gi, go,
     w_sem, x_send, x_recv, first_send, first_recv, halo_send, halo_recv, in_send, in_recv, out_send, out_recv, own_sem) = scratch
    tokens = rows * width
    part = tokens // nsh
    sub = part // subs
    crowd = nsh * sub
    rim = (rows + 2) * width
    me = lax.axis_index("shard")
    sec = lax.axis_index("section")
    side = lax.axis_index("halo")
    nxt = lax.rem(sec + 1, nsec)

    own = pltpu.make_async_copy(feat, FX, w_sem.at[7])
    own.start()
    loads = [
        pltpu.make_async_copy(src, dst, w_sem.at[i])
        for i, (src, dst) in enumerate(
            ((cf_h, cf), (cs_h, cs), (tw_h, tw), (qkv_h, qkv), (ao_h, ao), (gi_h, gi), (go_h, go))
        )
    ]
    for load in loads:
        load.start()

    def at(shard, section):
        return {"shard": shard, "section": section}

    barrier = pltpu.get_barrier_semaphore()
    peers = [{"halo": 1 - side}]
    for d in range(1, nsh):
        peers.append(at(lax.rem(me + d, nsh), sec))
    for e in sorted({1 % nsec, (nsec - 1) % nsec} - {0}):
        for d in range(nsh):
            peers.append(at(lax.rem(me + d, nsh), lax.rem(sec + e, nsec)))
        peers.append({"section": lax.rem(sec + e, nsec), "halo": 1 - side})
    for peer in peers:
        pl.semaphore_signal(barrier, inc=1, device_id=peer, device_id_type=MESH)
    pl.semaphore_wait(barrier, len(peers))

    edge_at = pl.multiple_of((1 - side) * (tokens - width), 16)
    piece = tokens // SHIFTS
    shifts = [
        pltpu.make_async_remote_copy(
            src_ref=feat.at[pl.ds(i * piece, piece)], dst_ref=F.at[0, pl.ds(i * piece, piece)],
            send_sem=x_send.at[i], recv_sem=x_recv.at[i],
            device_id={"section": nxt}, device_id_type=MESH,
        )
        for i in range(SHIFTS)
    ]
    firsts = [
        pltpu.make_async_remote_copy(
            src_ref=src, dst_ref=dst, send_sem=first_send.at[i], recv_sem=first_recv.at[i],
            device_id={"section": nxt, "halo": core}, device_id_type=MESH,
        )
        for i, (src, dst, core) in enumerate((
            (stat_tx.at[0], first_rx.at[0], side),
            (stat_tx.at[0], first_rx.at[1], 1 - side),
            (feat.at[pl.ds(edge_at, width)], edge_x.at[0], 1 - side),
        ))
    ]
    firsts[2].start()
    for i in range(SHIFTS // 2):
        shifts[i].start()
    stat_tx[...] = jnp.zeros_like(stat_tx)

    def fold(carry, v):
        s1, s2 = carry
        v = v.reshape(v.shape[0] // 8, 8, chans)
        return s1 + jnp.sum(v, axis=0), s2 + jnp.sum(v * v, axis=0)

    none = (jnp.zeros((8, chans), F32), jnp.zeros((8, chans), F32))

    def publish(slot, sums):
        stat_tx[slot, 0:1, :] = jnp.sum(sums[0], axis=0, keepdims=True)
        stat_tx[slot, 1:2, :] = jnp.sum(sums[1], axis=0, keepdims=True)

    own.wait()

    def own_total(i, carry):
        return fold(carry, FX[pl.ds(pl.multiple_of(i * BLK, BLK), BLK), :].astype(F32))
    publish(0, lax.fori_loop(0, tokens // BLK, own_total, none, unroll=UNROLL))
    firsts[0].start()
    firsts[1].start()
    for i in range(SHIFTS // 2, SHIFTS):
        shifts[i].start()

    per = chans // GROUPS
    ci = lax.broadcasted_iota(jnp.int32, (chans, chans), 0)
    cj = lax.broadcasted_iota(jnp.int32, (chans, chans), 1)
    gmask[...] = jnp.where(ci - lax.rem(ci, per) == cj - lax.rem(cj, per), 1.0, 0.0).astype(F32)
    lanes = hmask.shape[1]
    hi_ = lax.broadcasted_iota(jnp.int32, (chans, lanes), 0)
    hj_ = lax.broadcasted_iota(jnp.int32, (chans, lanes), 1)
    hmask[...] = jnp.where(hi_ - lax.rem(hi_, HEAD_DIM) == hj_ * HEAD_DIM, HEAD_DIM ** (-0.5), 0.0).astype(BF16)
    ti_ = lax.broadcasted_iota(jnp.int32, (lanes, chans), 0)
    tj_ = lax.broadcasted_iota(jnp.int32, (lanes, chans), 1)
    hmask_t[...] = jnp.where(tj_ - lax.rem(tj_, HEAD_DIM) == ti_ * HEAD_DIM, 1.0, 0.0).astype(BF16)
    zeros_rim = jnp.zeros((width, chans), F32)
    G[pl.ds(0, PAD), :] = jnp.zeros((PAD, chans), F32)
    G[pl.ds(PAD + rim, PAD), :] = jnp.zeros((PAD, chans), F32)
    G[pl.ds(PAD, width), :] = zeros_rim
    G[pl.ds(PAD + rim - width, width), :] = zeros_rim

    loads[2].wait()
    half = chans // 2
    lane = lax.broadcasted_iota(jnp.int32, (16, chans), 1)
    k_of = jnp.where(lane < half, lane, lane - half).astype(F32)
    frequency = jnp.exp(-math.log(10000.0) * k_of / half)
    for n in range(STEPS):
        angles = stamps[0, n].astype(F32) * frequency
        wave = jnp.where(lane < half, jnp.cos(angles), jnp.sin(angles))
        emb[n] = matmul(silu(wave).astype(BF16), tw[...])

    rim_at = pl.multiple_of(PAD + (1 - side) * (rim - width), 8)
    count = float(rows * 2 * width * per)

    def swap(slot, edge_src, edge_dst):
        copies = [
            pltpu.make_async_remote_copy(
                src_ref=src, dst_ref=dst, send_sem=halo_send.at[slot, i], recv_sem=halo_recv.at[slot, i],
                device_id={"halo": 1 - side}, device_id_type=MESH,
            )
            for i, (src, dst) in enumerate(
                ((edge_src, edge_dst), (stat_tx.at[slot], stat_rx.at[slot]))
            )
        ]
        return copies

    def moments(both):
        summed = jnp.dot(both, gmask[...], preferred_element_type=F32, precision=lax.Precision.HIGHEST)
        average = summed[0:1, :] / count
        second = summed[1:2, :] / count
        return average, lax.rsqrt(second - average * average + 1e-05)

    def activate(load, load_edge, both, arrivals=()):
        average, inverse = moments(both)

        def one(i, c):
            at_ = pl.multiple_of(i * BLK, BLK)
            G[pl.ds(PAD + width + at_, BLK), :] = silu((load(pl.ds(at_, BLK)) - average) * inverse)
            return c
        stages = max(len(arrivals), 1)
        for i in range(stages):
            if arrivals:
                arrivals[i].wait_recv()
            lax.fori_loop(i * (tokens // BLK) // stages, (i + 1) * (tokens // BLK) // stages, one, 0, unroll=2)
        G[pl.ds(rim_at, width), :] = silu((load_edge() - average) * inverse)
        col = lax.rem(lax.broadcasted_iota(jnp.int32, (width, chans), 0), width)

        def two(i, c):
            at_ = pl.multiple_of(i * width, width)
            window = G[pl.ds(at_, width + 2 * PAD), :]
            left = window[PAD - 1 : PAD - 1 + width]
            mid = window[PAD : PAD + width]
            right = window[PAD + 1 : PAD + 1 + width]
            dst = pl.ds(at_, width)
            A[dst, 0:chans] = jnp.where(col == 0, 0.0, left).astype(BF16)
            A[dst, chans : 2 * chans] = mid.astype(BF16)
            A[dst, 2 * chans :] = jnp.where(col == width - 1, 0.0, right).astype(BF16)
            return c
        lax.fori_loop(0, rows + 2, two, 0, unroll=5)

    def conv(weights, start, size):
        return sum(matmul(A[pl.ds(start + r * width, size), :], weights[r]) for r in range(3))

    def normalise(src):
        def one(i, c):
            at_ = pl.ds(pl.multiple_of(i * BLK, BLK), BLK)
            v = src(at_)
            centred = v - jnp.mean(v, axis=-1, keepdims=True)
            spread = jnp.mean(centred * centred, axis=-1, keepdims=True)
            N[at_, :] = (centred * lax.rsqrt(spread + 1e-05)).astype(BF16)
            return c
        lax.fori_loop(0, crowd // BLK, one, 0, unroll=UNROLL)

    def gather_copy(n, k, d):
        to = lax.rem(me + d, nsh)
        return pltpu.make_async_remote_copy(
            src_ref=S.at[n, k, to], dst_ref=PB.at[n, k, me],
            send_sem=in_send.at[n, k, d], recv_sem=in_recv.at[n, k, d],
            device_id={"shard": to}, device_id_type=MESH,
        )

    def return_copy(n, k, d):
        last = n == STEPS - 1
        target = out if last else F.at[n + 1]
        landing = target.at[pl.ds(pl.multiple_of(me * part + k * sub, 16), sub)]
        to = lax.rem(me + d, nsh)
        if d == 0 and (last or nsec == 1):
            return pltpu.make_async_copy(O.at[n, k, me], landing, own_sem.at[n, k])
        return pltpu.make_async_remote_copy(
            src_ref=O.at[n, k, to], dst_ref=landing,
            send_sem=out_send.at[n, k, d], recv_sem=out_recv.at[n, k, d],
            device_id=at(to, sec if last else nxt), device_id_type=MESH,
        )

    def pixels(n, k):
        stream = PB.at[n, k]

        def load_p(s):
            return stream.reshape(crowd, chans)[s, :].astype(F32)
        normalise(load_p)
        proj = matmul(N[...], qkv[...]).astype(BF16)
        Q[...] = proj[:, :chans].astype(F32)
        K[...] = proj[:, chans : 2 * chans].astype(F32)
        V[...] = proj[:, 2 * chans :].astype(F32)

        def frame(f, c):
            q = Q[pl.ds(pl.multiple_of(f * sub, 16), sub), :]
            start = pl.multiple_of(f * crowd, 16)
            for g in range(nsh):
                prod = q * K[g * sub : (g + 1) * sub, :]
                high = prod.astype(BF16)
                PH[pl.ds(start + g * sub, sub), :] = high
                PL[pl.ds(start + g * sub, sub), :] = (prod - high.astype(F32)).astype(BF16)
            score = matmul(PH[pl.ds(start, crowd), :], hmask[...]) + matmul(PL[pl.ds(start, crowd), :], hmask[...])
            pieces = [score[g * sub : (g + 1) * sub] for g in range(nsh)]
            top = functools.reduce(jnp.maximum, pieces)
            pieces = [jnp.exp(p - top) for p in pieces]
            scale = 1.0 / functools.reduce(jnp.add, pieces)
            weights = jnp.concatenate([(p * scale).astype(BF16) for p in pieces], axis=0)
            weights = matmul(weights, hmask_t[...])
            mixed = weights[0:sub] * V[0:sub, :]
            for g in range(1, nsh):
                mixed = mixed + weights[g * sub : (g + 1) * sub] * V[g * sub : (g + 1) * sub, :]
            OB[pl.ds(pl.multiple_of(f * sub, 16), sub), :] = mixed.astype(BF16)
            return c
        lax.fori_loop(0, nsh, frame, 0, unroll=4)

        S2[...] = (matmul(OB[...], ao[...]) + stream[...].reshape(crowd, chans).astype(F32)).astype(BF16)
        normalise(lambda s: S2[s, :].astype(F32))
        wide = 256
        for j in range(inner // wide):
            value = matmul(N[...], gi[:, j * wide : (j + 1) * wide])
            gate = matmul(N[...], gi[:, inner + j * wide : inner + (j + 1) * wide])
            gelu = 0.5 * gate * (1.0 + lax.erf(gate * (0.5 ** 0.5)))
            ACT[:, j * wide : (j + 1) * wide] = (value * gelu).astype(BF16)
        O[n, k] = (matmul_t(ACT[...], go[...]) + S2[...].astype(F32)).astype(BF16).reshape(nsh, sub, chans)

    for n in range(STEPS):
        field = F.at[n]

        def load_x(s, field=field):
            return field[s, :].astype(F32)

        if n == 0:
            for c in firsts:
                c.wait()
            activate(load_x, lambda: edge_x[0].astype(F32), first_rx[0] + first_rx[1], shifts)
            for c in shifts:
                c.wait_send()
            loads[0].wait()
        else:
            swaps = swap(2 * n, field.at[pl.ds(edge_at, width)], edge_x.at[n])
            swaps[0].start()
            publish(2 * n, sums)
            swaps[1].start()
            for c in swaps:
                c.wait()
            activate(load_x, lambda n=n: edge_x[n].astype(F32), stat_tx[2 * n] + stat_rx[2 * n])
        sums = none
        for i in range(2):
            rows_ = pl.ds(i * (tokens // 2), tokens // 2)
            h1 = conv(cf, i * (tokens // 2), tokens // 2) + emb[n, 0:1, :]
            H[n, rows_, :] = h1
            sums = fold(sums, h1)

        slot = 2 * n + 1
        swaps = swap(slot, H.at[n, pl.ds(edge_at, width)], edge_h.at[n])
        swaps[0].start()
        publish(slot, sums)
        swaps[1].start()
        for c in swaps:
            c.wait()
        activate(lambda s, n=n: H[n, s, :], lambda n=n: edge_h[n], stat_tx[slot] + stat_rx[slot])
        if n == 0:
            loads[1].wait()
        for k in range(subs):
            spans = [j * part + k * sub for j in range(nsh)]
            total = sum(
                matmul(jnp.concatenate([A[pl.ds(r * width + a, sub), :] for a in spans], axis=0), cs[r])
                for r in range(3)
            )
            base = jnp.concatenate([field[pl.ds(a, sub), :] for a in spans], axis=0)
            S[n, k] = (total + base.astype(F32)).astype(BF16).reshape(nsh, sub, chans)
            for d in range(1, nsh):
                gather_copy(n, k, d).start()
            PB[n, k, me] = S[n, k, me]

        if n == 0:
            for i in (3, 4, 5, 6):
                loads[i].wait()

        def temporal(k, carry, n=n):
            for d in range(1, nsh):
                gather_copy(n, k, d).wait_recv()
            pixels(n, k)
            for d in range(nsh):
                return_copy(n, k, d).start()
            return carry
        lax.fori_loop(0, subs, temporal, 0)

        sums = none
        for k in range(subs):
            for d in range(nsh):
                return_copy(n, k, d).wait()
            if n < STEPS - 1:
                for j in range(nsh):
                    sums = fold(sums, F[n + 1, pl.ds(j * part + k * sub, sub), :].astype(F32))
        for k in range(subs):
            for d in range(1, nsh):
                gather_copy(n, k, d).wait_send()


def slab_kernel(dims, stamps, feat, cf_h, cs_h, tw_h, qkv_h, ao_h, gi_h, go_h, out, *scratch):
    (rows, width, chans, inner, nsh, nsec, nha) = dims
    (FX, X, EX, H, HB, EH, GM, RM, S, S2, O, SI, ST_tx, ST_rx, S0, SC, SD, emb, gmask, hmask, hmask_t,
     N, Q, K, V, PH, PL, OB, FN, ACT, WC1, WC2, WN1, WN2, tw, qkv, ao, gi, go,
     w_sem, c_sem, init_send, init_recv, s0_send, s0_recv, st_send, st_recv, hx_send, hx_recv, hh_send, hh_recv,
     x_send, x_recv, out_send, out_recv, own_sem) = scratch
    R = nsh * nha
    q = rows // nsh
    T = q * width
    NF = nsh
    CH = 2 if NF % 2 == 0 else 1
    sub = T // 2
    crowd = NF * sub
    main = chans // 256 * 256
    rest = chans - main
    deep = 3 * main
    me = lax.axis_index("shard")
    sec = lax.axis_index("section")
    side = lax.axis_index("halo")
    r = me * nha + side
    nxt = lax.rem(sec + 1, nsec)
    has_up = r > 0
    has_down = r < R - 1

    own = pltpu.make_async_copy(feat, FX, w_sem.at[0])
    own.start()

    def peer(rr, section):
        return {"shard": lax.div(rr, nha), "halo": lax.rem(rr, nha), "section": section}

    barrier = pltpu.get_barrier_semaphore()
    peers = [peer(lax.rem(r + d, R), sec) for d in range(1, R)]
    for e in sorted({1 % nsec, (nsec - 1) % nsec} - {0}):
        for d in range(R):
            peers.append(peer(lax.rem(r + d, R), lax.rem(sec + e, nsec)))
    for p in peers:
        pl.semaphore_signal(barrier, inc=1, device_id=p, device_id_type=MESH)

    loads = [
        pltpu.make_async_copy(src, dst, w_sem.at[1 + i])
        for i, (src, dst) in enumerate(((tw_h, tw), (qkv_h, qkv), (ao_h, ao), (gi_h, gi), (go_h, go)))
    ]

    def conv_loads(src, dst, k):
        copies = []
        for t in range(3):
            copies.append(pltpu.make_async_copy(
                src.at[t, :, pl.ds(0, main), :], dst.at[:, pl.ds(t * main, main), :], c_sem.at[k, 2 * t]))
            copies.append(pltpu.make_async_copy(
                src.at[t, :, pl.ds(main, rest), :], dst.at[:, pl.ds(deep + t * rest, rest), :], c_sem.at[k, 2 * t + 1]))
        return copies

    first_loads = conv_loads(cf_h, WC1, 0)
    second_loads = conv_loads(cs_h, WC2, 1)
    loads[0].start()
    for c in first_loads + second_loads:
        c.start()
    for c in loads[1:]:
        c.start()
    pl.semaphore_wait(barrier, len(peers))

    def remote(src, dst, send, recv, device):
        return pltpu.make_async_remote_copy(
            src_ref=src, dst_ref=dst, send_sem=send, recv_sem=recv, device_id=device, device_id_type=MESH)

    def init_copy(j):
        return remote(feat.at[pl.ds(j * T, T)], X.at[0, me], init_send.at[j], init_recv.at[me],
                      peer(side * nsh + j, nxt))

    def init_wait(f):
        return remote(feat.at[pl.ds(0, T)], X.at[0, f], init_send.at[0], init_recv.at[f], peer(r, nxt))

    for j in range(nsh):
        init_copy(j).start()

    def start_sums(v):
        v = v.reshape(v.shape[0] // 8, 8, v.shape[1])
        return jnp.sum(v, axis=0), jnp.sum(v * v, axis=0)

    own.wait()
    none = jnp.zeros((8, chans), F32)

    def own_total(i, carry):
        s1, s2 = start_sums(FX[pl.ds(pl.multiple_of(i * BLK, BLK), BLK), :].astype(F32))
        return carry[0] + s1, carry[1] + s2
    s1, s2 = lax.fori_loop(0, rows * width // BLK, own_total, (none, none), unroll=UNROLL)
    S0[0:1, :] = jnp.sum(s1, axis=0, keepdims=True)
    S0[1:2, :] = jnp.sum(s2, axis=0, keepdims=True)

    def s0_copy(d):
        return remote(S0, SI.at[me, side], s0_send.at[d], s0_recv.at[me, side], peer(lax.rem(r + d, R), nxt))

    def s0_wait(f, h):
        return remote(S0, SI.at[f, h], s0_send.at[0], s0_recv.at[f, h], peer(r, nxt))

    for d in range(R):
        s0_copy(d).start()

    per = chans // GROUPS
    ci = lax.broadcasted_iota(jnp.int32, (chans, chans), 0)
    cj = lax.broadcasted_iota(jnp.int32, (chans, chans), 1)
    gmask[...] = jnp.where(ci - lax.rem(ci, per) == cj - lax.rem(cj, per), 1.0, 0.0).astype(BF16)
    lanes = hmask.shape[1]
    hi_ = lax.broadcasted_iota(jnp.int32, (chans, lanes), 0)
    hj_ = lax.broadcasted_iota(jnp.int32, (chans, lanes), 1)
    hmask[...] = jnp.where(hi_ - lax.rem(hi_, HEAD_DIM) == hj_ * HEAD_DIM, HEAD_DIM ** (-0.5), 0.0).astype(BF16)
    ti_ = lax.broadcasted_iota(jnp.int32, (lanes, chans), 0)
    tj_ = lax.broadcasted_iota(jnp.int32, (lanes, chans), 1)
    hmask_t[...] = jnp.where(tj_ - lax.rem(tj_, HEAD_DIM) == ti_ * HEAD_DIM, 1.0, 0.0).astype(BF16)
    SC[...] = jnp.zeros_like(SC)

    loads[0].wait()
    half = chans // 2
    lane = lax.broadcasted_iota(jnp.int32, (16, chans), 1)
    k_of = jnp.where(lane < half, lane, lane - half).astype(F32)
    frequency = jnp.exp(-math.log(10000.0) * k_of / half)
    for n in range(STEPS):
        angles = stamps[0, n].astype(F32) * frequency
        wave = jnp.where(lane < half, jnp.cos(angles), jnp.sin(angles))
        emb[n] = matmul(silu(wave).astype(BF16), tw[...])

    def pack(WC, WN):
        WN[:, 0:rest] = WC[0, :, main:]
        WN[:, rest:2 * rest] = WC[2, :, main:]
        WN[:, 2 * rest:3 * rest] = WC[1, :, main:]
        WN[:, 3 * rest:] = jnp.zeros((3 * chans, WN.shape[1] - 3 * rest), BF16)

    for c in first_loads:
        c.wait()
    pack(WC1, WN1)
    for c in second_loads:
        c.wait()
    pack(WC2, WN2)

    count = float(rows * nha * width * per)

    def stat_copy(slot, f, d, section):
        return remote(ST_tx.at[slot, f], ST_rx.at[slot, f, d], st_send.at[slot, f, d], st_recv.at[slot, f, d],
                      peer(lax.rem(r + d, R), section))

    def edge_x(n, f, way):
        src = X.at[n, f, pl.ds(way * (T - width), width)]
        return remote(src, EX.at[n, 1 - way, f], hx_send.at[n, way, f], hx_recv.at[n, 1 - way, f],
                      peer(jnp.clip(r + 2 * way - 1, 0, R - 1), sec))

    def edge_h(n, c, way):
        span = pl.ds(c * CH, CH)
        return remote(HB.at[n, way, span], EH.at[n, 1 - way, span], hh_send.at[n, way, c], hh_recv.at[n, 1 - way, c],
                      peer(jnp.clip(r + 2 * way - 1, 0, R - 1), sec))

    def on_edges(act, up, down):
        @pl.when(has_up)
        def _():
            act(up)

        @pl.when(has_down)
        def _():
            act(down)

    def start(copies):
        for c in copies:
            c.start()

    def wait_recv(copies):
        for c in copies:
            c.wait_recv()

    def wait_send(copies):
        for c in copies:
            c.wait_send()

    def scales(totals):
        for i, tot in enumerate(totals):
            high = tot.astype(BF16).astype(F32)
            left = tot - high
            mid = left.astype(BF16).astype(F32)
            for p, v in enumerate((high, mid, left - mid)):
                SC[2 * (p * CH + i):2 * (p * CH + i) + 2, :] = v
        SD[...] = matmul(SC[...].astype(BF16), gmask[...])
        got = []
        for i in range(CH):
            def row(j, i=i):
                return sum(SD[2 * (p * CH + i) + j:2 * (p * CH + i) + j + 1, :] for p in range(3)) / count
            average, second = row(0), row(1)
            got.append((average, 0.5 * lax.rsqrt(second - average * average + 1e-05)))
        return got

    def glow(v, average, slope):
        u = (v - average) * slope
        return u + u * jnp.tanh(u)

    up_big = jnp.full((width, main), r, jnp.int32)
    up_small = jnp.full((width, rest), r, jnp.int32)

    def activate(f, load, average, slope):
        tails = []
        for i in range(q + 2):
            big = glow(load(i, 0, main), average[:, :main], slope[:, :main])
            small = glow(load(i, main, rest), average[:, main:], slope[:, main:])
            if i == 0:
                big = jnp.where(up_big > 0, big, 0.0)
                small = jnp.where(up_small > 0, small, 0.0)
            if i == q + 1:
                big = jnp.where(up_big < R - 1, big, 0.0)
                small = jnp.where(up_small < R - 1, small, 0.0)
            GM[f, pl.ds(i * width, width), :] = big.astype(BF16)
            tails.append(small.astype(BF16))
        for o in range(q):
            for t in range(3):
                RM[f, pl.ds(o * width, width), t * rest:(t + 1) * rest] = tails[o + t]

    def conv(WC, WN, c):
        size = CH * T
        lhs = jnp.concatenate([
            jnp.concatenate([GM[f, pl.ds(t * width, T), :] for t in range(3)] + [RM[f]], axis=1)
            for f in range(c * CH, (c + 1) * CH)
        ], axis=0)
        col = lax.rem(lax.broadcasted_iota(jnp.int32, (size, main), 0), width)
        left = jnp.where(col == 0, 0.0, pltpu.roll(matmul(lhs, WC[0, :, 0:main]), 1, 0))
        right = jnp.where(col == width - 1, 0.0, pltpu.roll(matmul(lhs, WC[2, :, 0:main]), size - 1, 0))
        big = matmul(lhs, WC[1, :, 0:main]) + left + right
        last = matmul(lhs, WN[...])
        col = lax.rem(lax.broadcasted_iota(jnp.int32, last.shape, 0), width)
        left = jnp.where(col == 0, 0.0, pltpu.roll(last, 1, 0))
        right = jnp.where(col == width - 1, 0.0, pltpu.roll(last, size - 1, 0))
        small = last[:, 2 * rest:3 * rest] + left[:, 0:rest] + right[:, rest:2 * rest]
        return big, small

    def put_sums(slot, f, v, a, b):
        s1, s2 = start_sums(v)
        ST_tx[slot, f, 0:1, a:b] = jnp.sum(s1, axis=0, keepdims=True)
        ST_tx[slot, f, 1:2, a:b] = jnp.sum(s2, axis=0, keepdims=True)

    def layer_norm(v):
        centred = v - jnp.mean(v, axis=-1, keepdims=True)
        spread = jnp.mean(centred * centred, axis=-1, keepdims=True)
        return (centred * lax.rsqrt(spread + 1e-05)).astype(BF16)

    def attend(k, carry):
        at = pl.ds(pl.multiple_of(k * sub, 16), sub)
        for f in range(NF):
            N[f * sub:(f + 1) * sub, :] = layer_norm(S[f, at, :].astype(F32))
        proj = matmul(N[...], qkv[...]).astype(BF16)
        Q[...] = proj[:, :chans].astype(F32)
        K[...] = proj[:, chans:2 * chans].astype(F32)
        V[...] = proj[:, 2 * chans:].astype(F32)

        def frame(f, c):
            qf = Q[pl.ds(pl.multiple_of(f * sub, 16), sub), :]
            base = pl.multiple_of(f * crowd, 16)
            for g in range(NF):
                prod = qf * K[g * sub:(g + 1) * sub, :]
                high = prod.astype(BF16)
                PH[pl.ds(base + g * sub, sub), :] = high
                PL[pl.ds(base + g * sub, sub), :] = (prod - high.astype(F32)).astype(BF16)
            score = matmul(PH[pl.ds(base, crowd), :], hmask[...]) + matmul(PL[pl.ds(base, crowd), :], hmask[...])
            pieces = [score[g * sub:(g + 1) * sub] for g in range(NF)]
            top = functools.reduce(jnp.maximum, pieces)
            pieces = [jnp.exp(p - top) for p in pieces]
            scale = 1.0 / functools.reduce(jnp.add, pieces)
            weights = jnp.concatenate([(p * scale).astype(BF16) for p in pieces], axis=0)
            weights = matmul(weights, hmask_t[...])
            mixed = weights[0:sub] * V[0:sub, :]
            for g in range(1, NF):
                mixed = mixed + weights[g * sub:(g + 1) * sub] * V[g * sub:(g + 1) * sub, :]
            OB[pl.ds(pl.multiple_of(f * sub, 16), sub), :] = mixed.astype(BF16)
            return c
        lax.fori_loop(0, NF, frame, 0, unroll=NF)
        mixed = matmul(OB[...], ao[...])
        for f in range(NF):
            S2[f, at, :] = (mixed[f * sub:(f + 1) * sub] + S[f, at, :].astype(F32)).astype(BF16)
        return carry

    def feed(n, f):
        FN[...] = layer_norm(S2[f].astype(F32))
        wide = 256
        for j in range(inner // wide):
            value = matmul(FN[...], gi[:, j * wide:(j + 1) * wide])
            gate = matmul(FN[...], gi[:, inner + j * wide:inner + (j + 1) * wide])
            gelu = 0.5 * gate * (1.0 + lax.erf(gate * (0.5 ** 0.5)))
            ACT[:, j * wide:(j + 1) * wide] = (value * gelu).astype(BF16)
        made = (matmul_t(ACT[...], go[...]) + S2[f].astype(F32)).astype(BF16)
        O[n, f] = made
        return made

    def x_copy(f):
        return remote(O.at[0, f], X.at[1, f], x_send.at[f], x_recv.at[f], peer(r, nxt))

    target = lax.div(r, nsh)
    piece = lax.rem(r, nsh)

    def out_copy(f):
        return remote(O.at[STEPS - 1, f], out.at[pl.ds(pl.multiple_of(piece * T, 16), T)],
                      out_send.at[f], out_recv.at[piece], {"shard": f, "halo": target})

    def out_local(f):
        return pltpu.make_async_copy(O.at[STEPS - 1, f], out.at[pl.ds(pl.multiple_of(piece * T, 16), T)], own_sem)

    def is_own(f):
        return jnp.logical_and(f == me, target == side)

    for n in range(STEPS):
        for f in range(NF):
            if n == 0:
                init_wait(f).wait_recv()
            else:
                x_copy(f).wait_recv()
            on_edges(start, [edge_x(n, f, 0)], [edge_x(n, f, 1)])

        for c in range(NF // CH):
            frames = range(c * CH, (c + 1) * CH)
            totals = []
            for f in frames:
                if n == 0:
                    for h in range(nha):
                        s0_wait(f, h).wait_recv()
                    totals.append(functools.reduce(jnp.add, [SI[f, h] for h in range(nha)]))
                else:
                    for d in range(R):
                        stat_copy(1, f, d, nxt).wait_recv()
                    totals.append(functools.reduce(jnp.add, [ST_rx[1, f, d] for d in range(R)]))
            found = scales(totals)
            on_edges(wait_recv, [edge_x(n, f, 1) for f in frames], [edge_x(n, f, 0) for f in frames])
            for f, (average, slope) in zip(frames, found):
                def load(i, a, size, f=f):
                    if 0 < i <= q:
                        return X[n, f, pl.ds((i - 1) * width, width), a:a + size].astype(F32)
                    return EX[n, 0 if i == 0 else 1, f, :, a:a + size].astype(F32)
                activate(f, load, average, slope)
            big, small = conv(WC1, WN1, c)
            big = big + emb[n, 0:1, 0:main]
            small = small + emb[n, 0:1, main:]
            slot = 0 if n == 0 else 2
            for i, f in enumerate(frames):
                for v, a, b in ((big[i * T:(i + 1) * T], 0, main), (small[i * T:(i + 1) * T], main, chans)):
                    H[f, :, a:b] = v
                    HB[n, 0, f, :, a:b] = v[0:width].astype(BF16)
                    HB[n, 1, f, :, a:b] = v[T - width:].astype(BF16)
                    put_sums(slot, f, v, a, b)
            on_edges(start, [edge_h(n, c, 0)], [edge_h(n, c, 1)])
            for f in frames:
                for d in range(1, R):
                    stat_copy(slot, f, d, sec).start()

        for c in range(NF // CH):
            frames = range(c * CH, (c + 1) * CH)
            totals = []
            for f in frames:
                for d in range(1, R):
                    stat_copy(slot, f, d, sec).wait_recv()
                totals.append(functools.reduce(
                    jnp.add, [ST_tx[slot, f]] + [ST_rx[slot, f, d] for d in range(1, R)]))
            found = scales(totals)
            on_edges(wait_recv, [edge_h(n, c, 1)], [edge_h(n, c, 0)])
            for f, (average, slope) in zip(frames, found):
                def load(i, a, size, f=f):
                    if 0 < i <= q:
                        return H[f, pl.ds((i - 1) * width, width), a:a + size]
                    return EH[n, 0 if i == 0 else 1, f, :, a:a + size].astype(F32)
                activate(f, load, average, slope)
            big, small = conv(WC2, WN2, c)
            for i, f in enumerate(frames):
                for v, a, b in ((big[i * T:(i + 1) * T], 0, main), (small[i * T:(i + 1) * T], main, chans)):
                    S[f, :, a:b] = (v + X[n, f, :, a:b].astype(F32)).astype(BF16)

        if n == 0:
            for load in loads[1:]:
                load.wait()
        lax.fori_loop(0, T // sub, attend, 0)

        if n < STEPS - 1:
            def pass_on(f, carry):
                made = feed(0, f).astype(F32)
                x_copy(f).start()
                put_sums(1, f, made, 0, chans)
                for d in range(R):
                    stat_copy(1, f, d, nxt).start()
                return carry
            lax.fori_loop(0, NF, pass_on, 0)
        else:
            def hand_in(k, carry):
                f = lax.rem(me + 1 + k, NF)
                feed(STEPS - 1, f)

                @pl.when(is_own(f))
                def _():
                    out_local(f).start()

                @pl.when(jnp.logical_not(is_own(f)))
                def _():
                    out_copy(f).start()
                return carry
            lax.fori_loop(0, NF, hand_in, 0)

    for j in range(nsh):
        init_copy(j).wait_send()
    for d in range(R):
        s0_copy(d).wait_send()
    for n in range(STEPS):
        on_edges(wait_send, [edge_x(n, f, 0) for f in range(NF)], [edge_x(n, f, 1) for f in range(NF)])
        on_edges(wait_send, [edge_h(n, c, 0) for c in range(NF // CH)], [edge_h(n, c, 1) for c in range(NF // CH)])
    for f in range(NF):
        for d in range(1, R):
            stat_copy(0, f, d, sec).wait_send()
            stat_copy(2, f, d, sec).wait_send()
        for d in range(R):
            stat_copy(1, f, d, nxt).wait_send()
        x_copy(f).wait_send()

    for f in range(NF):
        @pl.when(is_own(f))
        def _():
            out_local(f).wait()

        @pl.when(jnp.logical_not(is_own(f)))
        def _():
            out_copy(f).wait_send()
    for j in range(nsh):
        @pl.when(side * nsh + j != r)
        def _():
            remote(O.at[STEPS - 1, 0], out.at[pl.ds(j * T, T)], out_send.at[0], out_recv.at[j],
                   {"halo": 1 - side}).wait_recv()


def slab_scratch(rows, width, chans, inner, nsh, nha):
    V = pltpu.VMEM
    D = pltpu.SemaphoreType.DMA
    R = nsh * nha
    q = rows // nsh
    T = q * width
    NF = nsh
    CH = 2 if NF % 2 == 0 else 1
    crowd = NF * (T // 2)
    main = chans // 256 * 256
    rest = chans - main
    return [
        V((rows * width, chans), BF16),
        V((STEPS, NF, T, chans), BF16),
        V((STEPS, 2, NF, width, chans), BF16),
        V((NF, T, chans), F32),
        V((STEPS, 2, NF, width, chans), BF16),
        V((STEPS, 2, NF, width, chans), BF16),
        V((NF, (q + 2) * width, main), BF16),
        V((NF, T, 3 * rest), BF16),
        V((NF, T, chans), BF16),
        V((NF, T, chans), BF16),
        V((STEPS, NF, T, chans), BF16),
        V((NF, nha, 2, chans), F32),
        V((3, NF, 2, chans), F32),
        V((3, NF, R, 2, chans), F32),
        V((2, chans), F32),
        V((16, chans), F32),
        V((16, chans), F32),
        V((STEPS, 16, chans), F32),
        V((chans, chans), BF16),
        V((chans, 128), BF16),
        V((128, chans), BF16),
        V((crowd, chans), BF16),
        V((crowd, chans), F32), V((crowd, chans), F32), V((crowd, chans), F32),
        V((NF * crowd, chans), BF16), V((NF * crowd, chans), BF16),
        V((crowd, chans), BF16), V((T, chans), BF16), V((T, inner), BF16),
        V((3, 3 * chans, chans), BF16), V((3, 3 * chans, chans), BF16),
        V((3 * chans, -(-3 * rest // 128) * 128), BF16), V((3 * chans, -(-3 * rest // 128) * 128), BF16),
        V((chans, chans), BF16), V((chans, 3 * chans), BF16), V((chans, chans), BF16),
        V((chans, 2 * inner), BF16), V((chans, inner), BF16),
        D((6,)), D((2, 6)), D((nsh,)), D((NF,)), D((R,)), D((NF, nha)), D((3, NF, R)), D((3, NF, R)),
        D((STEPS, 2, NF)), D((STEPS, 2, NF)), D((STEPS, 2, NF // CH)), D((STEPS, 2, NF // CH)),
        D((NF,)), D((NF,)), D((NF,)), D((nsh,)), D(()),
    ]


def solution(mesh):
    nsh, nsec, nha = mesh.shape["shard"], mesh.shape["section"], mesh.shape["halo"]

    def per_device(features, timesteps, conv_first, conv_second, time_weight, qkv_weight,
                   attn_out, geglu_in, geglu_out):
        _, _, rows, width, chans = features.shape
        inner = geglu_out.shape[1]
        tokens = rows * width
        any_ = pl.BlockSpec(memory_space=pl.ANY)
        if nsec > 1 and nha == 2 and rows % nsh == 0 and chans > 256 and chans % 256 and rows // nsh * width % 32 == 0:
            result = pl.pallas_call(
                functools.partial(slab_kernel, (rows, width, chans, inner, nsh, nsec, nha)),
                out_shape=jax.ShapeDtypeStruct((tokens, chans), BF16),
                in_specs=[pl.BlockSpec(memory_space=pltpu.SMEM)] + [any_] * 8,
                out_specs=any_,
                scratch_shapes=slab_scratch(rows, width, chans, inner, nsh, nha),
                compiler_params=pltpu.CompilerParams(
                    collective_id=0, has_side_effects=True, vmem_limit_bytes=60 * 1024 * 1024
                ),
            )(
                timesteps,
                features.reshape(tokens, chans),
                conv_first.reshape(3, 3, chans, chans),
                conv_second.reshape(3, 3, chans, chans),
                time_weight[0], qkv_weight[0], attn_out[0], geglu_in[0], jnp.swapaxes(geglu_out[0], 0, 1),
            )
            return result.reshape(features.shape)
        part = tokens // nsh
        rim = (rows + 2) * width
        subs = min(SUBS, part // 16)
        dims = (rows, width, chans, inner, nsh, nsec, subs)
        sub = part // subs
        crowd = nsh * sub
        V = pltpu.VMEM
        D = pltpu.SemaphoreType.DMA
        scratch = [
            V((STEPS, tokens, chans), BF16),
            V((tokens, chans), BF16),
            V((2, 8, chans), F32),
            V((STEPS, tokens, chans), F32),
            V((rim + 2 * PAD, chans), F32),
            V((rim, 3 * chans), BF16),
            V((STEPS, subs, nsh, sub, chans), BF16),
            V((STEPS, subs, nsh, sub, chans), BF16),
            V((STEPS, subs, nsh, sub, chans), BF16),
            V((2 * STEPS, 8, chans), F32),
            V((2 * STEPS, 8, chans), F32),
            V((STEPS, width, chans), BF16),
            V((STEPS, width, chans), F32),
            V((STEPS, 16, chans), F32),
            V((chans, chans), F32),
            V((chans, 128), BF16),
            V((128, chans), BF16),
            V((crowd, chans), BF16),
            V((crowd, chans), F32), V((crowd, chans), F32), V((crowd, chans), F32),
            V((nsh * crowd, chans), BF16), V((nsh * crowd, chans), BF16),
            V((crowd, chans), BF16), V((crowd, chans), BF16), V((crowd, inner), BF16),
            V((3, 3 * chans, chans), BF16), V((3, 3 * chans, chans), BF16),
            V((chans, chans), BF16), V((chans, 3 * chans), BF16), V((chans, chans), BF16),
            V((chans, 2 * inner), BF16), V((chans, inner), BF16),
            D((8,)), D((SHIFTS,)), D((SHIFTS,)), D((3,)), D((3,)), D((2 * STEPS, 2)), D((2 * STEPS, 2)),
            D((STEPS, subs, nsh)), D((STEPS, subs, nsh)), D((STEPS, subs, nsh)), D((STEPS, subs, nsh)),
            D((STEPS, subs)),
        ]
        result = pl.pallas_call(
            functools.partial(kernel, dims),
            out_shape=jax.ShapeDtypeStruct((tokens, chans), BF16),
            in_specs=[pl.BlockSpec(memory_space=pltpu.SMEM)] + [any_] * 8,
            out_specs=any_,
            scratch_shapes=scratch,
            compiler_params=pltpu.CompilerParams(
                collective_id=0, has_side_effects=True, vmem_limit_bytes=60 * 1024 * 1024
            ),
        )(
            timesteps,
            features.reshape(tokens, chans),
            conv_first.reshape(3, 3 * chans, chans),
            conv_second.reshape(3, 3 * chans, chans),
            time_weight[0], qkv_weight[0], attn_out[0], geglu_in[0], jnp.swapaxes(geglu_out[0], 0, 1),
        )
        return result.reshape(features.shape)

    return jax.shard_map(
        per_device,
        mesh=mesh,
        in_specs=(
            P(("groups", "section"), "shard", "halo", None, None),
            P(("groups", "section"), None),
            P("section", None, None, None, None),
            P("section", None, None, None, None),
            P("section", None, None),
            P("section", None, None),
            P("section", None, None),
            P("section", None, None),
            P("section", None, None),
        ),
        out_specs=P(("groups", "section"), "shard", "halo", None, None),
        check_vma=False,
    )
```

```python
import functools
import math

import jax
import jax.numpy as jnp
from jax import lax
from jax.experimental import pallas as pl
from jax.experimental.pallas import tpu as pltpu
from jax.sharding import PartitionSpec as P

HEAD_DIM = 64
GROUPS = 32
STEPS = 2
MESH = pl.DeviceIdType.MESH
F32 = jnp.float32
BF16 = jnp.bfloat16
BLK = 64
SUBS = 2
UNROLL = 4
SHIFTS = 4


def matmul(a, b):
    return jnp.dot(a, b, preferred_element_type=F32)


def matmul_t(a, b):
    return lax.dot_general(a, b, (((1,), (1,)), ((), ())), preferred_element_type=F32)


def silu(u):
    return u * (1.0 / (1.0 + jnp.exp(-u)))


def kernel(dims, stamps, feat, cf_h, cs_h, tw_h, qkv_h, ao_h, gi_h, go_h, out, *scratch):
    (rows, width, chans, inner, nsh, nsec, subs) = dims
    (F, FX, first_rx, H, GM, RM, SC, SD, S, PB, O, stat_tx, stat_rx, edge_x, edge_h, emb, gmask, hmask, hmask_t,
     N, Q, K, V, PH, PL, OB, S2, ACT,
     cf, cs, cf_n, cs_n, tw, qkv, ao, gi, go,
     w_sem, c_sem, x_send, x_recv, first_send, first_recv, halo_send, halo_recv, in_send, in_recv, out_send, out_recv, own_sem) = scratch
    tokens = rows * width
    part = tokens // nsh
    sub = part // subs
    crowd = nsh * sub
    rim = (rows + 2) * width
    me = lax.axis_index("shard")
    sec = lax.axis_index("section")
    side = lax.axis_index("halo")
    nxt = lax.rem(sec + 1, nsec)

    main = chans // 256 * 256
    rest = chans - main
    own = pltpu.make_async_copy(feat, FX, w_sem.at[7])
    own.start()
    loads = [
        pltpu.make_async_copy(src, dst, w_sem.at[i])
        for i, (src, dst) in enumerate(
            ((tw_h, tw), (qkv_h, qkv), (ao_h, ao), (gi_h, gi), (go_h, go))
        )
    ]

    def conv_loads(src, dst, k):
        copies = []
        for t in range(3):
            copies.append(pltpu.make_async_copy(
                src.at[t, :, pl.ds(0, main), :], dst.at[:, pl.ds(t * main, main), :], c_sem.at[k, 2 * t]))
            copies.append(pltpu.make_async_copy(
                src.at[t, :, pl.ds(main, rest), :], dst.at[:, pl.ds(3 * main + t * rest, rest), :],
                c_sem.at[k, 2 * t + 1]))
        return copies

    first_loads = conv_loads(cf_h, cf, 0)
    second_loads = conv_loads(cs_h, cs, 1)
    for load in [loads[0]] + first_loads + second_loads + loads[1:]:
        load.start()

    def at(shard, section):
        return {"shard": shard, "section": section}

    barrier = pltpu.get_barrier_semaphore()
    peers = [{"halo": 1 - side}]
    for d in range(1, nsh):
        peers.append(at(lax.rem(me + d, nsh), sec))
    for e in sorted({1 % nsec, (nsec - 1) % nsec} - {0}):
        for d in range(nsh):
            peers.append(at(lax.rem(me + d, nsh), lax.rem(sec + e, nsec)))
        peers.append({"section": lax.rem(sec + e, nsec), "halo": 1 - side})
    for peer in peers:
        pl.semaphore_signal(barrier, inc=1, device_id=peer, device_id_type=MESH)
    pl.semaphore_wait(barrier, len(peers))

    edge_at = pl.multiple_of((1 - side) * (tokens - width), 16)
    piece = tokens // SHIFTS
    shifts = [
        pltpu.make_async_remote_copy(
            src_ref=feat.at[pl.ds(i * piece, piece)], dst_ref=F.at[0, pl.ds(i * piece, piece)],
            send_sem=x_send.at[i], recv_sem=x_recv.at[i],
            device_id={"section": nxt}, device_id_type=MESH,
        )
        for i in range(SHIFTS)
    ]
    firsts = [
        pltpu.make_async_remote_copy(
            src_ref=src, dst_ref=dst, send_sem=first_send.at[i], recv_sem=first_recv.at[i],
            device_id={"section": nxt, "halo": core}, device_id_type=MESH,
        )
        for i, (src, dst, core) in enumerate((
            (stat_tx.at[0], first_rx.at[0], side),
            (stat_tx.at[0], first_rx.at[1], 1 - side),
            (feat.at[pl.ds(edge_at, width)], edge_x.at[0], 1 - side),
        ))
    ]
    firsts[2].start()
    for i in range(SHIFTS // 2):
        shifts[i].start()
    stat_tx[...] = jnp.zeros_like(stat_tx)

    def fold(carry, v):
        s1, s2 = carry
        v = v.reshape(v.shape[0] // 8, 8, v.shape[1])
        return s1 + jnp.sum(v, axis=0), s2 + jnp.sum(v * v, axis=0)

    none = (jnp.zeros((8, chans), F32), jnp.zeros((8, chans), F32))

    def publish(slot, sums, a=0, b=chans):
        stat_tx[slot, 0:1, a:b] = jnp.sum(sums[0], axis=0, keepdims=True)
        stat_tx[slot, 1:2, a:b] = jnp.sum(sums[1], axis=0, keepdims=True)

    own.wait()

    def own_total(i, carry):
        return fold(carry, FX[pl.ds(pl.multiple_of(i * BLK, BLK), BLK), :].astype(F32))
    publish(0, lax.fori_loop(0, tokens // BLK, own_total, none, unroll=UNROLL))
    firsts[0].start()
    firsts[1].start()
    for i in range(SHIFTS // 2, SHIFTS):
        shifts[i].start()

    per = chans // GROUPS
    ci = lax.broadcasted_iota(jnp.int32, (chans, chans), 0)
    cj = lax.broadcasted_iota(jnp.int32, (chans, chans), 1)
    gmask[...] = jnp.where(ci - lax.rem(ci, per) == cj - lax.rem(cj, per), 1.0, 0.0).astype(BF16)
    lanes = hmask.shape[1]
    hi_ = lax.broadcasted_iota(jnp.int32, (chans, lanes), 0)
    hj_ = lax.broadcasted_iota(jnp.int32, (chans, lanes), 1)
    hmask[...] = jnp.where(hi_ - lax.rem(hi_, HEAD_DIM) == hj_ * HEAD_DIM, HEAD_DIM ** (-0.5), 0.0).astype(BF16)
    ti_ = lax.broadcasted_iota(jnp.int32, (lanes, chans), 0)
    tj_ = lax.broadcasted_iota(jnp.int32, (lanes, chans), 1)
    hmask_t[...] = jnp.where(tj_ - lax.rem(tj_, HEAD_DIM) == ti_ * HEAD_DIM, 1.0, 0.0).astype(BF16)
    for at_ in (0, rim - width):
        GM[pl.ds(at_, width), :] = jnp.zeros((width, main), BF16)
    SC[...] = jnp.zeros_like(SC)

    loads[0].wait()
    half = chans // 2
    lane = lax.broadcasted_iota(jnp.int32, (16, chans), 1)
    k_of = jnp.where(lane < half, lane, lane - half).astype(F32)
    frequency = jnp.exp(-math.log(10000.0) * k_of / half)
    for n in range(STEPS):
        angles = stamps[0, n].astype(F32) * frequency
        wave = jnp.where(lane < half, jnp.cos(angles), jnp.sin(angles))
        emb[n] = matmul(silu(wave).astype(BF16), tw[...])

    def pack(full, narrow):
        narrow[:, 0:rest] = full[0, :, main:]
        narrow[:, rest:2 * rest] = full[2, :, main:]
        narrow[:, 2 * rest:3 * rest] = full[1, :, main:]
        narrow[:, 3 * rest:] = jnp.zeros((3 * chans, narrow.shape[1] - 3 * rest), BF16)

    for c in first_loads:
        c.wait()
    pack(cf, cf_n)
    rim_at = pl.multiple_of((1 - side) * (rim - width), 16)
    count = float(rows * 2 * width * per)

    def swap(slot, edge_src, edge_dst):
        copies = [
            pltpu.make_async_remote_copy(
                src_ref=src, dst_ref=dst, send_sem=halo_send.at[slot, i], recv_sem=halo_recv.at[slot, i],
                device_id={"halo": 1 - side}, device_id_type=MESH,
            )
            for i, (src, dst) in enumerate(
                ((edge_src, edge_dst), (stat_tx.at[slot], stat_rx.at[slot]))
            )
        ]
        return copies

    def moments(both):
        high = both.astype(BF16).astype(F32)
        left = both - high
        mid = left.astype(BF16).astype(F32)
        for p, v in enumerate((high, mid, left - mid)):
            SC[2 * p:2 * p + 2, :] = v[0:2]
        SD[...] = matmul(SC[...].astype(BF16), gmask[...])
        average = (SD[0:1, :] + SD[2:3, :] + SD[4:5, :]) / count
        second = (SD[1:2, :] + SD[3:4, :] + SD[5:6, :]) / count
        return average, 0.5 * lax.rsqrt(second - average * average + 1e-05)

    def glow(v, average, slope):
        u = (v - average) * slope
        return u + u * jnp.tanh(u)

    below = jnp.full((width, rest), side, jnp.int32)

    def activate(load, load_edge, both, arrivals=()):
        average, slope = moments(both)
        stages = max(len(arrivals), 1)
        for i in range(rows):
            if arrivals and i % (rows // stages) == 0:
                arrivals[i // (rows // stages)].wait_recv()
            v = load(pl.ds(i * width, width))
            GM[pl.ds((i + 1) * width, width), :] = glow(v[:, :main], average[:, :main], slope[:, :main]).astype(BF16)
            small = glow(v[:, main:], average[:, main:], slope[:, main:]).astype(BF16)
            for t in range(3):
                if 0 <= i + 1 - t < rows:
                    RM[pl.ds((i + 1 - t) * width, width), t * rest:(t + 1) * rest] = small
        v = load_edge()
        GM[pl.ds(rim_at, width), :] = glow(v[:, :main], average[:, :main], slope[:, :main]).astype(BF16)
        small = glow(v[:, main:], average[:, main:], slope[:, main:])
        RM[pl.ds(0, width), 0:rest] = jnp.where(below > 0, small, 0.0).astype(BF16)
        RM[pl.ds((rows - 1) * width, width), 2 * rest:3 * rest] = jnp.where(below > 0, 0.0, small).astype(BF16)

    def conv(full, narrow, spans, size):
        lhs = jnp.concatenate([
            jnp.concatenate([GM[pl.ds(a + t * width, size), :] for t in range(3)] + [RM[pl.ds(a, size), :]], axis=1)
            for a in spans
        ], axis=0)
        many = size * len(spans)

        def shifted(y, by):
            col = lax.rem(lax.broadcasted_iota(jnp.int32, y.shape, 0), width)
            return jnp.where(col == (0 if by == 1 else width - 1), 0.0, pltpu.roll(y, by, 0))
        big = (matmul(lhs, full[1, :, 0:main]) + shifted(matmul(lhs, full[0, :, 0:main]), 1)
               + shifted(matmul(lhs, full[2, :, 0:main]), many - 1))
        last = matmul(lhs, narrow[...])
        small = (last[:, 2 * rest:3 * rest] + shifted(last, 1)[:, 0:rest]
                 + shifted(last, many - 1)[:, rest:2 * rest])
        return big, small

    def normalise(src):
        def one(i, c):
            at_ = pl.ds(pl.multiple_of(i * BLK, BLK), BLK)
            v = src(at_)
            centred = v - jnp.mean(v, axis=-1, keepdims=True)
            spread = jnp.mean(centred * centred, axis=-1, keepdims=True)
            N[at_, :] = (centred * lax.rsqrt(spread + 1e-05)).astype(BF16)
            return c
        lax.fori_loop(0, crowd // BLK, one, 0, unroll=UNROLL)

    def gather_copy(n, k, d):
        to = lax.rem(me + d, nsh)
        return pltpu.make_async_remote_copy(
            src_ref=S.at[n, k, to], dst_ref=PB.at[n, k, me],
            send_sem=in_send.at[n, k, d], recv_sem=in_recv.at[n, k, d],
            device_id={"shard": to}, device_id_type=MESH,
        )

    def return_copy(n, k, d):
        last = n == STEPS - 1
        target = out if last else F.at[n + 1]
        landing = target.at[pl.ds(pl.multiple_of(me * part + k * sub, 16), sub)]
        to = lax.rem(me + d, nsh)
        if d == 0 and (last or nsec == 1):
            return pltpu.make_async_copy(O.at[n, k, me], landing, own_sem.at[n, k])
        return pltpu.make_async_remote_copy(
            src_ref=O.at[n, k, to], dst_ref=landing,
            send_sem=out_send.at[n, k, d], recv_sem=out_recv.at[n, k, d],
            device_id=at(to, sec if last else nxt), device_id_type=MESH,
        )

    def pixels(n, k):
        stream = PB.at[n, k]

        def load_p(s):
            return stream.reshape(crowd, chans)[s, :].astype(F32)
        normalise(load_p)
        proj = matmul(N[...], qkv[...]).astype(BF16)
        Q[...] = proj[:, :chans].astype(F32)
        K[...] = proj[:, chans : 2 * chans].astype(F32)
        V[...] = proj[:, 2 * chans :].astype(F32)

        def frame(f, c):
            q = Q[pl.ds(pl.multiple_of(f * sub, 16), sub), :]
            start = pl.multiple_of(f * crowd, 16)
            for g in range(nsh):
                prod = q * K[g * sub : (g + 1) * sub, :]
                high = prod.astype(BF16)
                PH[pl.ds(start + g * sub, sub), :] = high
                PL[pl.ds(start + g * sub, sub), :] = (prod - high.astype(F32)).astype(BF16)
            score = matmul(PH[pl.ds(start, crowd), :], hmask[...]) + matmul(PL[pl.ds(start, crowd), :], hmask[...])
            pieces = [score[g * sub : (g + 1) * sub] for g in range(nsh)]
            top = functools.reduce(jnp.maximum, pieces)
            pieces = [jnp.exp(p - top) for p in pieces]
            scale = 1.0 / functools.reduce(jnp.add, pieces)
            weights = jnp.concatenate([(p * scale).astype(BF16) for p in pieces], axis=0)
            weights = matmul(weights, hmask_t[...])
            mixed = weights[0:sub] * V[0:sub, :]
            for g in range(1, nsh):
                mixed = mixed + weights[g * sub : (g + 1) * sub] * V[g * sub : (g + 1) * sub, :]
            OB[pl.ds(pl.multiple_of(f * sub, 16), sub), :] = mixed.astype(BF16)
            return c
        lax.fori_loop(0, nsh, frame, 0, unroll=4)

        S2[...] = (matmul(OB[...], ao[...]) + stream[...].reshape(crowd, chans).astype(F32)).astype(BF16)
        normalise(lambda s: S2[s, :].astype(F32))
        wide = 256
        for j in range(inner // wide):
            value = matmul(N[...], gi[:, j * wide : (j + 1) * wide])
            gate = matmul(N[...], gi[:, inner + j * wide : inner + (j + 1) * wide])
            gelu = 0.5 * gate * (1.0 + lax.erf(gate * (0.5 ** 0.5)))
            ACT[:, j * wide : (j + 1) * wide] = (value * gelu).astype(BF16)
        O[n, k] = (matmul_t(ACT[...], go[...]) + S2[...].astype(F32)).astype(BF16).reshape(nsh, sub, chans)

    for n in range(STEPS):
        field = F.at[n]

        def load_x(s, field=field):
            return field[s, :].astype(F32)

        if n == 0:
            for c in firsts:
                c.wait()
            activate(load_x, lambda: edge_x[0].astype(F32), first_rx[0] + first_rx[1], shifts)
            for c in shifts:
                c.wait_send()
        else:
            swaps = swap(2 * n, field.at[pl.ds(edge_at, width)], edge_x.at[n])
            swaps[0].start()
            publish(2 * n, sums)
            swaps[1].start()
            for c in swaps:
                c.wait()
            activate(load_x, lambda n=n: edge_x[n].astype(F32), stat_tx[2 * n] + stat_rx[2 * n])
        big_sums = (jnp.zeros((8, main), F32), jnp.zeros((8, main), F32))
        small_sums = (jnp.zeros((8, rest), F32), jnp.zeros((8, rest), F32))
        for i in range(2):
            rows_ = pl.ds(i * (tokens // 2), tokens // 2)
            big, small = conv(cf, cf_n, [i * (tokens // 2)], tokens // 2)
            big = big + emb[n, 0:1, 0:main]
            small = small + emb[n, 0:1, main:]
            H[n, rows_, 0:main] = big
            H[n, rows_, main:] = small
            big_sums = fold(big_sums, big)
            small_sums = fold(small_sums, small)

        slot = 2 * n + 1
        swaps = swap(slot, H.at[n, pl.ds(edge_at, width)], edge_h.at[n])
        swaps[0].start()
        publish(slot, big_sums, 0, main)
        publish(slot, small_sums, main, chans)
        swaps[1].start()
        for c in swaps:
            c.wait()
        activate(lambda s, n=n: H[n, s, :], lambda n=n: edge_h[n], stat_tx[slot] + stat_rx[slot])
        if n == 0:
            for c in second_loads:
                c.wait()
            pack(cs, cs_n)
        whole_rows = sub % width == 0
        for k in range(subs):
            if whole_rows:
                spans, size = [j * part + k * sub for j in range(nsh)], sub
            else:
                spans, size = [k * (tokens // subs)], tokens // subs
            big, small = conv(cs, cs_n, spans, size)
            for i, a in enumerate(spans):
                for b in range(0, size, sub):
                    at_ = a + b
                    line = slice(i * size + b, i * size + b + sub)
                    to, kk = at_ // part, at_ % part // sub
                    for v, lo, hi in ((big[line], 0, main), (small[line], main, chans)):
                        S[n, kk, to, :, lo:hi] = (v + field[pl.ds(at_, sub), lo:hi].astype(F32)).astype(BF16)
            if whole_rows:
                for d in range(1, nsh):
                    gather_copy(n, k, d).start()
                PB[n, k, me] = S[n, k, me]
        if not whole_rows:
            for k in range(subs):
                for d in range(1, nsh):
                    gather_copy(n, k, d).start()
                PB[n, k, me] = S[n, k, me]

        if n == 0:
            for i in (1, 2, 3, 4):
                loads[i].wait()

        def temporal(k, carry, n=n):
            for d in range(1, nsh):
                gather_copy(n, k, d).wait_recv()
            pixels(n, k)
            for d in range(nsh):
                return_copy(n, k, d).start()
            return carry
        lax.fori_loop(0, subs, temporal, 0)

        sums = none
        for k in range(subs):
            for d in range(nsh):
                return_copy(n, k, d).wait()
            if n < STEPS - 1:
                for j in range(nsh):
                    sums = fold(sums, F[n + 1, pl.ds(j * part + k * sub, sub), :].astype(F32))
        for k in range(subs):
            for d in range(1, nsh):
                gather_copy(n, k, d).wait_send()


def solution(mesh):
    nsh, nsec = mesh.shape["shard"], mesh.shape["section"]

    def per_device(features, timesteps, conv_first, conv_second, time_weight, qkv_weight,
                   attn_out, geglu_in, geglu_out):
        _, _, rows, width, chans = features.shape
        inner = geglu_out.shape[1]
        tokens = rows * width
        part = tokens // nsh
        rim = (rows + 2) * width
        subs = min(SUBS, part // 16)
        dims = (rows, width, chans, inner, nsh, nsec, subs)
        sub = part // subs
        crowd = nsh * sub
        main = chans // 256 * 256
        rest = chans - main
        any_ = pl.BlockSpec(memory_space=pl.ANY)
        V = pltpu.VMEM
        D = pltpu.SemaphoreType.DMA
        scratch = [
            V((STEPS, tokens, chans), BF16),
            V((tokens, chans), BF16),
            V((2, 8, chans), F32),
            V((STEPS, tokens, chans), F32),
            V((rim, main), BF16),
            V((tokens, 3 * rest), BF16),
            V((16, chans), F32),
            V((16, chans), F32),
            V((STEPS, subs, nsh, sub, chans), BF16),
            V((STEPS, subs, nsh, sub, chans), BF16),
            V((STEPS, subs, nsh, sub, chans), BF16),
            V((2 * STEPS, 8, chans), F32),
            V((2 * STEPS, 8, chans), F32),
            V((STEPS, width, chans), BF16),
            V((STEPS, width, chans), F32),
            V((STEPS, 16, chans), F32),
            V((chans, chans), BF16),
            V((chans, 128), BF16),
            V((128, chans), BF16),
            V((crowd, chans), BF16),
            V((crowd, chans), F32), V((crowd, chans), F32), V((crowd, chans), F32),
            V((nsh * crowd, chans), BF16), V((nsh * crowd, chans), BF16),
            V((crowd, chans), BF16), V((crowd, chans), BF16), V((crowd, inner), BF16),
            V((3, 3 * chans, chans), BF16), V((3, 3 * chans, chans), BF16),
            V((3 * chans, -(-3 * rest // 128) * 128), BF16), V((3 * chans, -(-3 * rest // 128) * 128), BF16),
            V((chans, chans), BF16), V((chans, 3 * chans), BF16), V((chans, chans), BF16),
            V((chans, 2 * inner), BF16), V((chans, inner), BF16),
            D((8,)), D((2, 6)), D((SHIFTS,)), D((SHIFTS,)), D((3,)), D((3,)), D((2 * STEPS, 2)), D((2 * STEPS, 2)),
            D((STEPS, subs, nsh)), D((STEPS, subs, nsh)), D((STEPS, subs, nsh)), D((STEPS, subs, nsh)),
            D((STEPS, subs)),
        ]
        result = pl.pallas_call(
            functools.partial(kernel, dims),
            out_shape=jax.ShapeDtypeStruct((tokens, chans), BF16),
            in_specs=[pl.BlockSpec(memory_space=pltpu.SMEM)] + [any_] * 8,
            out_specs=any_,
            scratch_shapes=scratch,
            compiler_params=pltpu.CompilerParams(
                collective_id=0, has_side_effects=True, vmem_limit_bytes=60 * 1024 * 1024
            ),
        )(
            timesteps,
            features.reshape(tokens, chans),
            conv_first.reshape(3, 3, chans, chans),
            conv_second.reshape(3, 3, chans, chans),
            time_weight[0], qkv_weight[0], attn_out[0], geglu_in[0], jnp.swapaxes(geglu_out[0], 0, 1),
        )
        return result.reshape(features.shape)

    return jax.shard_map(
        per_device,
        mesh=mesh,
        in_specs=(
            P(("groups", "section"), "shard", "halo", None, None),
            P(("groups", "section"), None),
            P("section", None, None, None, None),
            P("section", None, None, None, None),
            P("section", None, None),
            P("section", None, None),
            P("section", None, None),
            P("section", None, None),
            P("section", None, None),
        ),
        out_specs=P(("groups", "section"), "shard", "halo", None, None),
        check_vma=False,
    )
```

```python
import functools
import math

import jax
import jax.numpy as jnp
from jax import lax
from jax.experimental import pallas as pl
from jax.experimental.pallas import tpu as pltpu
from jax.sharding import PartitionSpec as P

HEAD_DIM = 64
GROUPS = 32
STEPS = 2
MESH = pl.DeviceIdType.MESH
F32 = jnp.float32
BF16 = jnp.bfloat16
BLK = 64
SUBS = 2
UNROLL = 4
SHIFTS = 4


def matmul(a, b):
    return jnp.dot(a, b, preferred_element_type=F32)


def matmul_t(a, b):
    return lax.dot_general(a, b, (((1,), (1,)), ((), ())), preferred_element_type=F32)


def silu(u):
    return u * (1.0 / (1.0 + jnp.exp(-u)))


def kernel(dims, stamps, feat, cf_h, cs_h, tw_h, qkv_h, ao_h, gi_h, go_h, out, *scratch):
    (rows, width, chans, inner, nsh, nsec, subs) = dims
    (F, FX, first_rx, H, GM, RM, SC, SD, S, PB, O, stat_tx, stat_rx, edge_x, edge_h, emb, gmask, gather, spread,
     N, Q, K, V, K4, V4, PP, W, OB, S2, ACT,
     cf, cs, cf_n, cs_n, tw, qkv, ao, gi, go,
     w_sem, c_sem, x_send, x_recv, first_send, first_recv, halo_send, halo_recv, in_send, in_recv, out_send, out_recv, own_sem) = scratch
    tokens = rows * width
    part = tokens // nsh
    sub = part // subs
    crowd = nsh * sub
    rim = (rows + 2) * width
    me = lax.axis_index("shard")
    sec = lax.axis_index("section")
    side = lax.axis_index("halo")
    nxt = lax.rem(sec + 1, nsec)

    main = chans // 256 * 256
    rest = chans - main
    own = pltpu.make_async_copy(feat, FX, w_sem.at[7])
    own.start()
    loads = [
        pltpu.make_async_copy(src, dst, w_sem.at[i])
        for i, (src, dst) in enumerate(
            ((tw_h, tw), (qkv_h, qkv), (ao_h, ao), (gi_h, gi), (go_h, go))
        )
    ]

    def conv_loads(src, dst, k):
        copies = []
        for t in range(3):
            copies.append(pltpu.make_async_copy(
                src.at[t, :, pl.ds(0, main), :], dst.at[:, pl.ds(t * main, main), :], c_sem.at[k, 2 * t]))
            copies.append(pltpu.make_async_copy(
                src.at[t, :, pl.ds(main, rest), :], dst.at[:, pl.ds(3 * main + t * rest, rest), :],
                c_sem.at[k, 2 * t + 1]))
        return copies

    first_loads = conv_loads(cf_h, cf, 0)
    second_loads = conv_loads(cs_h, cs, 1)
    for load in [loads[0]] + first_loads + second_loads + loads[1:]:
        load.start()

    def at(shard, section):
        return {"shard": shard, "section": section}

    barrier = pltpu.get_barrier_semaphore()
    peers = [{"halo": 1 - side}]
    for d in range(1, nsh):
        peers.append(at(lax.rem(me + d, nsh), sec))
    for e in sorted({1 % nsec, (nsec - 1) % nsec} - {0}):
        for d in range(nsh):
            peers.append(at(lax.rem(me + d, nsh), lax.rem(sec + e, nsec)))
        peers.append({"section": lax.rem(sec + e, nsec), "halo": 1 - side})
    for peer in peers:
        pl.semaphore_signal(barrier, inc=1, device_id=peer, device_id_type=MESH)
    pl.semaphore_wait(barrier, len(peers))

    edge_at = pl.multiple_of((1 - side) * (tokens - width), 16)
    piece = tokens // SHIFTS
    shifts = [
        pltpu.make_async_remote_copy(
            src_ref=feat.at[pl.ds(i * piece, piece)], dst_ref=F.at[0, pl.ds(i * piece, piece)],
            send_sem=x_send.at[i], recv_sem=x_recv.at[i],
            device_id={"section": nxt}, device_id_type=MESH,
        )
        for i in range(SHIFTS)
    ]
    firsts = [
        pltpu.make_async_remote_copy(
            src_ref=src, dst_ref=dst, send_sem=first_send.at[i], recv_sem=first_recv.at[i],
            device_id={"section": nxt, "halo": core}, device_id_type=MESH,
        )
        for i, (src, dst, core) in enumerate((
            (stat_tx.at[0], first_rx.at[0], side),
            (stat_tx.at[0], first_rx.at[1], 1 - side),
            (feat.at[pl.ds(edge_at, width)], edge_x.at[0], 1 - side),
        ))
    ]
    firsts[2].start()
    for i in range(SHIFTS // 2):
        shifts[i].start()
    stat_tx[...] = jnp.zeros_like(stat_tx)

    def fold(carry, v):
        s1, s2 = carry
        v = v.reshape(v.shape[0] // 8, 8, v.shape[1])
        return s1 + jnp.sum(v, axis=0), s2 + jnp.sum(v * v, axis=0)

    none = (jnp.zeros((8, chans), F32), jnp.zeros((8, chans), F32))

    def publish(slot, sums, a=0, b=chans):
        stat_tx[slot, 0:1, a:b] = jnp.sum(sums[0], axis=0, keepdims=True)
        stat_tx[slot, 1:2, a:b] = jnp.sum(sums[1], axis=0, keepdims=True)

    own.wait()

    def own_total(i, carry):
        return fold(carry, FX[pl.ds(pl.multiple_of(i * BLK, BLK), BLK), :].astype(F32))
    publish(0, lax.fori_loop(0, tokens // BLK, own_total, none, unroll=UNROLL))
    firsts[0].start()
    firsts[1].start()
    for i in range(SHIFTS // 2, SHIFTS):
        shifts[i].start()

    per = chans // GROUPS
    ci = lax.broadcasted_iota(jnp.int32, (chans, chans), 0)
    cj = lax.broadcasted_iota(jnp.int32, (chans, chans), 1)
    gmask[...] = jnp.where(ci - lax.rem(ci, per) == cj - lax.rem(cj, per), 1.0, 0.0).astype(BF16)
    lanes = gather.shape[1]
    step = lanes // nsh
    heads = main // HEAD_DIM
    tall = nsh * main
    row_ = lax.broadcasted_iota(jnp.int32, (main, lanes), 0)
    row_ = row_ - lax.rem(row_, HEAD_DIM)
    col_ = lax.broadcasted_iota(jnp.int32, (main, lanes), 1)
    down = lax.broadcasted_iota(jnp.int32, (lanes, main), 0)
    over = lax.broadcasted_iota(jnp.int32, (lanes, main), 1)
    over = over - lax.rem(over, HEAD_DIM)
    for g in range(nsh):
        hit = row_ == (col_ - g * step) * HEAD_DIM
        gather[g * main:(g + 1) * main, :] = jnp.where(hit, HEAD_DIM ** (-0.5), 0.0).astype(BF16)
        hit = col_[0:rest] == g * step + heads
        gather[tall + g * rest:tall + (g + 1) * rest, :] = jnp.where(hit, HEAD_DIM ** (-0.5), 0.0).astype(BF16)
        spread[:, g * main:(g + 1) * main] = jnp.where(over == (down - g * step) * HEAD_DIM, 1.0, 0.0).astype(BF16)
    for j in range(nsh * rest // lanes):
        low = jnp.where(over[:, 0:lanes] < HEAD_DIM, 0, step)
        hit = down[:, 0:lanes] - (j * lanes // rest * step + heads) == low
        spread[:, tall + j * lanes:tall + (j + 1) * lanes] = jnp.where(hit, 1.0, 0.0).astype(BF16)
    for at_ in (0, rim - width):
        GM[pl.ds(at_, width), :] = jnp.zeros((width, main), BF16)
    SC[...] = jnp.zeros_like(SC)

    loads[0].wait()
    half = chans // 2
    lane = lax.broadcasted_iota(jnp.int32, (16, chans), 1)
    k_of = jnp.where(lane < half, lane, lane - half).astype(F32)
    frequency = jnp.exp(-math.log(10000.0) * k_of / half)
    for n in range(STEPS):
        angles = stamps[0, n].astype(F32) * frequency
        wave = jnp.where(lane < half, jnp.cos(angles), jnp.sin(angles))
        emb[n] = matmul(silu(wave).astype(BF16), tw[...])

    def pack(full, narrow):
        narrow[:, 0:rest] = full[0, :, main:]
        narrow[:, rest:2 * rest] = full[2, :, main:]
        narrow[:, 2 * rest:3 * rest] = full[1, :, main:]
        narrow[:, 3 * rest:] = jnp.zeros((3 * chans, narrow.shape[1] - 3 * rest), BF16)

    for c in first_loads:
        c.wait()
    pack(cf, cf_n)
    rim_at = pl.multiple_of((1 - side) * (rim - width), 16)
    count = float(rows * 2 * width * per)

    def swap(slot, edge_src, edge_dst):
        copies = [
            pltpu.make_async_remote_copy(
                src_ref=src, dst_ref=dst, send_sem=halo_send.at[slot, i], recv_sem=halo_recv.at[slot, i],
                device_id={"halo": 1 - side}, device_id_type=MESH,
            )
            for i, (src, dst) in enumerate(
                ((edge_src, edge_dst), (stat_tx.at[slot], stat_rx.at[slot]))
            )
        ]
        return copies

    def moments(both):
        high = both.astype(BF16).astype(F32)
        left = both - high
        mid = left.astype(BF16).astype(F32)
        for p, v in enumerate((high, mid, left - mid)):
            SC[2 * p:2 * p + 2, :] = v[0:2]
        SD[...] = matmul(SC[...].astype(BF16), gmask[...])
        average = (SD[0:1, :] + SD[2:3, :] + SD[4:5, :]) / count
        second = (SD[1:2, :] + SD[3:4, :] + SD[5:6, :]) / count
        return average, 0.5 * lax.rsqrt(second - average * average + 1e-05)

    def glow(v, average, slope):
        u = (v - average) * slope
        return u + u * jnp.tanh(u)

    below = jnp.full((width, rest), side, jnp.int32)

    def activate(load, load_edge, both, arrivals=()):
        average, slope = moments(both)
        stages = max(len(arrivals), 1)
        for i in range(rows):
            if arrivals and i % (rows // stages) == 0:
                arrivals[i // (rows // stages)].wait_recv()
            v = load(pl.ds(i * width, width))
            GM[pl.ds((i + 1) * width, width), :] = glow(v[:, :main], average[:, :main], slope[:, :main]).astype(BF16)
            small = glow(v[:, main:], average[:, main:], slope[:, main:]).astype(BF16)
            for t in range(3):
                if 0 <= i + 1 - t < rows:
                    RM[pl.ds((i + 1 - t) * width, width), t * rest:(t + 1) * rest] = small
        v = load_edge()
        GM[pl.ds(rim_at, width), :] = glow(v[:, :main], average[:, :main], slope[:, :main]).astype(BF16)
        small = glow(v[:, main:], average[:, main:], slope[:, main:])
        RM[pl.ds(0, width), 0:rest] = jnp.where(below > 0, small, 0.0).astype(BF16)
        RM[pl.ds((rows - 1) * width, width), 2 * rest:3 * rest] = jnp.where(below > 0, 0.0, small).astype(BF16)

    def conv(full, narrow, spans, size):
        lhs = jnp.concatenate([
            jnp.concatenate([GM[pl.ds(a + t * width, size), :] for t in range(3)] + [RM[pl.ds(a, size), :]], axis=1)
            for a in spans
        ], axis=0)
        many = size * len(spans)

        def shifted(y, by):
            col = lax.rem(lax.broadcasted_iota(jnp.int32, y.shape, 0), width)
            return jnp.where(col == (0 if by == 1 else width - 1), 0.0, pltpu.roll(y, by, 0))
        big = (matmul(lhs, full[1, :, 0:main]) + shifted(matmul(lhs, full[0, :, 0:main]), 1)
               + shifted(matmul(lhs, full[2, :, 0:main]), many - 1))
        last = matmul(lhs, narrow[...])
        small = (last[:, 2 * rest:3 * rest] + shifted(last, 1)[:, 0:rest]
                 + shifted(last, many - 1)[:, rest:2 * rest])
        return big, small

    def normalise(src):
        def one(i, c):
            at_ = pl.ds(pl.multiple_of(i * BLK, BLK), BLK)
            v = src(at_)
            centred = v - jnp.mean(v, axis=-1, keepdims=True)
            spread = jnp.mean(centred * centred, axis=-1, keepdims=True)
            N[at_, :] = (centred * lax.rsqrt(spread + 1e-05)).astype(BF16)
            return c
        lax.fori_loop(0, crowd // BLK, one, 0, unroll=UNROLL)

    def gather_copy(n, k, d):
        to = lax.rem(me + d, nsh)
        return pltpu.make_async_remote_copy(
            src_ref=S.at[n, k, to], dst_ref=PB.at[n, k, me],
            send_sem=in_send.at[n, k, d], recv_sem=in_recv.at[n, k, d],
            device_id={"shard": to}, device_id_type=MESH,
        )

    def return_copy(n, k, d):
        last = n == STEPS - 1
        target = out if last else F.at[n + 1]
        landing = target.at[pl.ds(pl.multiple_of(me * part + k * sub, 16), sub)]
        to = lax.rem(me + d, nsh)
        if d == 0 and (last or nsec == 1):
            return pltpu.make_async_copy(O.at[n, k, me], landing, own_sem.at[n, k])
        return pltpu.make_async_remote_copy(
            src_ref=O.at[n, k, to], dst_ref=landing,
            send_sem=out_send.at[n, k, d], recv_sem=out_recv.at[n, k, d],
            device_id=at(to, sec if last else nxt), device_id_type=MESH,
        )

    def pixels(n, k):
        stream = PB.at[n, k]

        def load_p(s):
            return stream.reshape(crowd, chans)[s, :].astype(F32)
        normalise(load_p)
        proj = matmul(N[...], qkv[...]).astype(BF16)
        Q[...] = proj[:, :chans].astype(F32)
        K[...] = proj[:, chans : 2 * chans].astype(F32)
        V[...] = proj[:, 2 * chans :].astype(F32)

        for g in range(nsh):
            K4[:, g * rest:(g + 1) * rest] = K[g * sub:(g + 1) * sub, main:]
            V4[:, g * rest:(g + 1) * rest] = V[g * sub:(g + 1) * sub, main:]

        def products(f, c):
            at_ = pl.multiple_of(f * sub, 16)
            q = Q[pl.ds(at_, sub), :]
            tail = jnp.concatenate([q[:, main:]] * (lanes // rest), axis=1)

            def put(v, a):
                high = v.astype(BF16)
                PP[pl.ds(at_, sub), a:a + v.shape[1]] = high
                PP[pl.ds(crowd + at_, sub), a:a + v.shape[1]] = (v - high.astype(F32)).astype(BF16)
            for g in range(nsh):
                put(q[:, :main] * K[g * sub:(g + 1) * sub, :main], g * main)
            for a in range(0, nsh * rest, lanes):
                put(tail * K4[:, a:a + lanes], tall + a)
            return c
        lax.fori_loop(0, nsh, products, 0, unroll=4)
        score = matmul(PP[...], gather[...])
        score = score[:crowd] + score[crowd:]

        def across(fold_, v):
            turn = step
            while turn < lanes:
                v = fold_(v, pltpu.roll(v, turn, 1))
                turn *= 2
            return v
        score = jnp.exp(score - across(jnp.maximum, score))
        W[...] = (score * (1.0 / across(jnp.add, score))).astype(BF16)
        weights = matmul(W[...], spread[...])
        for f in range(nsh):
            mine = weights[f * sub:(f + 1) * sub]
            mixed = mine[:, :main] * V[0:sub, :main]
            for g in range(1, nsh):
                mixed = mixed + mine[:, g * main:(g + 1) * main] * V[g * sub:(g + 1) * sub, :main]
            OB[f * sub:(f + 1) * sub, :main] = mixed.astype(BF16)
            tail = mine[:, tall:tall + lanes] * V4[:, 0:lanes]
            for a in range(lanes, nsh * rest, lanes):
                tail = tail + mine[:, tall + a:tall + a + lanes] * V4[:, a:a + lanes]
            tail = tail + pltpu.roll(tail, rest, 1)
            OB[f * sub:(f + 1) * sub, main:] = tail[:, :rest].astype(BF16)

        S2[...] = (matmul(OB[...], ao[...]) + stream[...].reshape(crowd, chans).astype(F32)).astype(BF16)
        normalise(lambda s: S2[s, :].astype(F32))
        wide = 256
        for j in range(inner // wide):
            value = matmul(N[...], gi[:, j * wide : (j + 1) * wide])
            gate = matmul(N[...], gi[:, inner + j * wide : inner + (j + 1) * wide])
            gelu = 0.5 * gate * (1.0 + lax.erf(gate * (0.5 ** 0.5)))
            ACT[:, j * wide : (j + 1) * wide] = (value * gelu).astype(BF16)
        O[n, k] = (matmul_t(ACT[...], go[...]) + S2[...].astype(F32)).astype(BF16).reshape(nsh, sub, chans)

    for n in range(STEPS):
        field = F.at[n]

        def load_x(s, field=field):
            return field[s, :].astype(F32)

        if n == 0:
            for c in firsts:
                c.wait()
            activate(load_x, lambda: edge_x[0].astype(F32), first_rx[0] + first_rx[1], shifts)
            for c in shifts:
                c.wait_send()
        else:
            swaps = swap(2 * n, field.at[pl.ds(edge_at, width)], edge_x.at[n])
            swaps[0].start()
            publish(2 * n, sums)
            swaps[1].start()
            for c in swaps:
                c.wait()
            activate(load_x, lambda n=n: edge_x[n].astype(F32), stat_tx[2 * n] + stat_rx[2 * n])
        big_sums = (jnp.zeros((8, main), F32), jnp.zeros((8, main), F32))
        small_sums = (jnp.zeros((8, rest), F32), jnp.zeros((8, rest), F32))
        for i in range(2):
            rows_ = pl.ds(i * (tokens // 2), tokens // 2)
            big, small = conv(cf, cf_n, [i * (tokens // 2)], tokens // 2)
            big = big + emb[n, 0:1, 0:main]
            small = small + emb[n, 0:1, main:]
            H[n, rows_, 0:main] = big
            H[n, rows_, main:] = small
            big_sums = fold(big_sums, big)
            small_sums = fold(small_sums, small)

        slot = 2 * n + 1
        swaps = swap(slot, H.at[n, pl.ds(edge_at, width)], edge_h.at[n])
        swaps[0].start()
        publish(slot, big_sums, 0, main)
        publish(slot, small_sums, main, chans)
        swaps[1].start()
        for c in swaps:
            c.wait()
        activate(lambda s, n=n: H[n, s, :], lambda n=n: edge_h[n], stat_tx[slot] + stat_rx[slot])
        if n == 0:
            for c in second_loads:
                c.wait()
            pack(cs, cs_n)
        whole_rows = sub % width == 0
        for k in range(subs):
            if whole_rows:
                spans, size = [j * part + k * sub for j in range(nsh)], sub
            else:
                spans, size = [k * (tokens // subs)], tokens // subs
            big, small = conv(cs, cs_n, spans, size)
            for i, a in enumerate(spans):
                for b in range(0, size, sub):
                    at_ = a + b
                    line = slice(i * size + b, i * size + b + sub)
                    to, kk = at_ // part, at_ % part // sub
                    for v, lo, hi in ((big[line], 0, main), (small[line], main, chans)):
                        S[n, kk, to, :, lo:hi] = (v + field[pl.ds(at_, sub), lo:hi].astype(F32)).astype(BF16)
            if whole_rows:
                for d in range(1, nsh):
                    gather_copy(n, k, d).start()
                PB[n, k, me] = S[n, k, me]
        if not whole_rows:
            for k in range(subs):
                for d in range(1, nsh):
                    gather_copy(n, k, d).start()
                PB[n, k, me] = S[n, k, me]

        if n == 0:
            for i in (1, 2, 3, 4):
                loads[i].wait()

        def temporal(k, carry, n=n):
            for d in range(1, nsh):
                gather_copy(n, k, d).wait_recv()
            pixels(n, k)
            for d in range(nsh):
                return_copy(n, k, d).start()
            return carry
        lax.fori_loop(0, subs, temporal, 0)

        sums = none
        for k in range(subs):
            for d in range(nsh):
                return_copy(n, k, d).wait()
            if n < STEPS - 1:
                for j in range(nsh):
                    sums = fold(sums, F[n + 1, pl.ds(j * part + k * sub, sub), :].astype(F32))
        for k in range(subs):
            for d in range(1, nsh):
                gather_copy(n, k, d).wait_send()


def solution(mesh):
    nsh, nsec = mesh.shape["shard"], mesh.shape["section"]

    def per_device(features, timesteps, conv_first, conv_second, time_weight, qkv_weight,
                   attn_out, geglu_in, geglu_out):
        _, _, rows, width, chans = features.shape
        inner = geglu_out.shape[1]
        tokens = rows * width
        part = tokens // nsh
        rim = (rows + 2) * width
        subs = min(SUBS, part // 16)
        dims = (rows, width, chans, inner, nsh, nsec, subs)
        sub = part // subs
        crowd = nsh * sub
        main = chans // 256 * 256
        rest = chans - main
        any_ = pl.BlockSpec(memory_space=pl.ANY)
        V = pltpu.VMEM
        D = pltpu.SemaphoreType.DMA
        scratch = [
            V((STEPS, tokens, chans), BF16),
            V((tokens, chans), BF16),
            V((2, 8, chans), F32),
            V((STEPS, tokens, chans), F32),
            V((rim, main), BF16),
            V((tokens, 3 * rest), BF16),
            V((16, chans), F32),
            V((16, chans), F32),
            V((STEPS, subs, nsh, sub, chans), BF16),
            V((STEPS, subs, nsh, sub, chans), BF16),
            V((STEPS, subs, nsh, sub, chans), BF16),
            V((2 * STEPS, 8, chans), F32),
            V((2 * STEPS, 8, chans), F32),
            V((STEPS, width, chans), BF16),
            V((STEPS, width, chans), F32),
            V((STEPS, 16, chans), F32),
            V((chans, chans), BF16),
            V((nsh * chans, 128), BF16),
            V((128, nsh * chans), BF16),
            V((crowd, chans), BF16),
            V((crowd, chans), F32), V((crowd, chans), F32), V((crowd, chans), F32),
            V((sub, nsh * rest), F32), V((sub, nsh * rest), F32),
            V((2 * crowd, nsh * chans), BF16), V((crowd, 128), BF16),
            V((crowd, chans), BF16), V((crowd, chans), BF16), V((crowd, inner), BF16),
            V((3, 3 * chans, chans), BF16), V((3, 3 * chans, chans), BF16),
            V((3 * chans, -(-3 * rest // 128) * 128), BF16), V((3 * chans, -(-3 * rest // 128) * 128), BF16),
            V((chans, chans), BF16), V((chans, 3 * chans), BF16), V((chans, chans), BF16),
            V((chans, 2 * inner), BF16), V((chans, inner), BF16),
            D((8,)), D((2, 6)), D((SHIFTS,)), D((SHIFTS,)), D((3,)), D((3,)), D((2 * STEPS, 2)), D((2 * STEPS, 2)),
            D((STEPS, subs, nsh)), D((STEPS, subs, nsh)), D((STEPS, subs, nsh)), D((STEPS, subs, nsh)),
            D((STEPS, subs)),
        ]
        result = pl.pallas_call(
            functools.partial(kernel, dims),
            out_shape=jax.ShapeDtypeStruct((tokens, chans), BF16),
            in_specs=[pl.BlockSpec(memory_space=pltpu.SMEM)] + [any_] * 8,
            out_specs=any_,
            scratch_shapes=scratch,
            compiler_params=pltpu.CompilerParams(
                collective_id=0, has_side_effects=True, vmem_limit_bytes=60 * 1024 * 1024
            ),
        )(
            timesteps,
            features.reshape(tokens, chans),
            conv_first.reshape(3, 3, chans, chans),
            conv_second.reshape(3, 3, chans, chans),
            time_weight[0], qkv_weight[0], attn_out[0], geglu_in[0], jnp.swapaxes(geglu_out[0], 0, 1),
        )
        return result.reshape(features.shape)

    return jax.shard_map(
        per_device,
        mesh=mesh,
        in_specs=(
            P(("groups", "section"), "shard", "halo", None, None),
            P(("groups", "section"), None),
            P("section", None, None, None, None),
            P("section", None, None, None, None),
            P("section", None, None),
            P("section", None, None),
            P("section", None, None),
            P("section", None, None),
            P("section", None, None),
        ),
        out_specs=P(("groups", "section"), "shard", "halo", None, None),
        check_vma=False,
    )
```
